128 devices in a mesh: rep: 32 (over x, z, core), layer: 4 (over y).
Axes of the slice: x: 4, y: 4, z: 4, core: 2. Of those that a mesh axis runs over, the one named last changes fastest.
Arguments:
- activations: bfloat16 [4, 16384, 8192], P('layer', 'rep'), may hold values from -6 to 6
- output_grads: bfloat16 [4, 16384, 8192], P('layer', 'rep'), may hold values from -6 to 6
- in_projection: bfloat16 [4, 32, 8192], P('layer'), may hold values from -0.0625 to 0.0625
- out_projection: bfloat16 [4, 32, 8192], P('layer'), may hold values from -0.0625 to 0.0625
- segment_ids: int32 [16384], P('rep'), may hold values from -1 to 61, as said below
- move_list: int32 [1984], P('rep'), may hold values from -1 to 1023, as said below
Outputs:
- factor: float32 [4, 1024, 1024], P('layer')
- features: bfloat16 [4, 1024, 1024], P('layer', 'rep')
- self_influence: float32 [1024], P('rep')
The draws below stay inside these ranges and needn't reach their ends.
Inputs may be any that keep to these rules, and one draw needn't show every extreme that they name: `segment_ids`: within each replica's 512 tokens the values never fall; a run of equal values is one document; -1 marks tokens continuing the previous replica's last document and never occurs on replica 0; n documents start on a replica with values 0 to n - 1, n from 2 to 62, and some replica has exactly 62; all documents together are 1024; the last document ends at the end of the last replica. `move_list`: replica r's block of 62 entries gives for its documents in order of their first token (the one continuing onto replica r + 1 included) the destination row in 0 to 1023, and -1 past its last document; every row is named exactly once; the documents of replica r go to rows of replica r - 1, r or r + 1 (rows m * 32 to m * 32 + 31 belong to replica m).
All inputs are finite; a program needn't handle non-finite values.
Results may differ from the reference program's by a relative error of at most 0.0064.
Values may be sent and summed in bfloat16 or wider, within the bound.
A program may use at most 128 MiB of HBM per device.

```python
import jax
import jax.numpy as jnp
from jax import lax

D = 8192
KIN = 32
KOUT = 32
TOK_DEV = 512
BAL = 32
DSLOT = 62
LAYERS = 4
TOKENS = 16384
DOCS = 1024
N_REP = 32


def make_plan(key):
    base = jax.random.fold_in(key, 11)
    key_drift, key_peak, key_place, key_rows = jax.random.split(base, 4)
    spread = BAL // 2 - 1
    drifts = jax.random.randint(key_drift, (N_REP + 1,), -spread, spread + 1)
    peak_rep = jax.random.randint(key_peak, (), 1, N_REP - 1)
    edge_idx = jnp.arange(N_REP + 1, dtype=jnp.int32)
    drifts = jnp.where(edge_idx == peak_rep, -spread, drifts)
    drifts = jnp.where(edge_idx == peak_rep + 1, spread, drifts)
    drifts = jnp.where((edge_idx == 0) | (edge_idx == N_REP), 0, drifts)
    doc_counts = BAL + drifts[1:] - drifts[:-1]
    place_keys = jax.random.split(key_place, N_REP)
    shuffled = jax.vmap(lambda subkey: jax.random.permutation(subkey, TOK_DEV))(place_keys)
    ranking = jnp.argsort(shuffled, axis=1).astype(jnp.int32)
    rank_zero = ranking[:, :1]
    token_pos = jnp.arange(TOK_DEV, dtype=jnp.int32)[None, :]
    moved_rank = jnp.where(token_pos == 0, 0, ranking + (ranking < rank_zero).astype(jnp.int32))
    rep_index = jnp.arange(N_REP, dtype=jnp.int32)[:, None]
    ranking = jnp.where(rep_index == 0, moved_rank, ranking)
    starts = ranking < doc_counts[:, None]
    segment = jnp.cumsum(starts.astype(jnp.int32), axis=1) - 1
    first_doc = jnp.arange(N_REP, dtype=jnp.int32) * BAL + drifts[:-1]
    doc_slot = jnp.arange(DSLOT, dtype=jnp.int32)[None, :]
    global_id = first_doc[:, None] + doc_slot
    row_keys = jax.random.split(key_rows, N_REP)
    inner_rows = jax.vmap(lambda subkey: jax.random.permutation(subkey, BAL))(row_keys).astype(jnp.int32)

    def natural_target(doc_ids):
        dest_rep = jnp.clip(doc_ids // BAL, 0, N_REP - 1)
        inside = jnp.clip(doc_ids - dest_rep * BAL, 0, BAL - 1)
        return dest_rep * BAL + inner_rows[dest_rep, inside]
    reps = jnp.arange(N_REP, dtype=jnp.int32)
    low_own = reps * BAL + jnp.maximum(drifts[:-1], 0)
    high_own = (reps + 1) * BAL - 1 + jnp.minimum(drifts[1:], 0)
    next_low = jnp.concatenate([low_own[1:], low_own[:1]])
    prev_high = jnp.concatenate([high_own[-1:], high_own[:-1]])
    rep_col = reps[:, None]
    target = natural_target(global_id)
    to_right = (global_id == high_own[:, None]) & (rep_col < N_REP - 1)
    to_left = (global_id == low_own[:, None]) & (rep_col > 0)
    target = jnp.where(to_right, natural_target(next_low)[:, None], target)
    target = jnp.where(to_left, natural_target(prev_high)[:, None], target)
    moves = jnp.where(doc_slot < doc_counts[:, None], target, -1)
    return (segment.reshape(-1).astype(jnp.int32), moves.reshape(-1).astype(jnp.int32))


def draw_segment_ids(key, part):
    segment, moves = make_plan(key)
    return segment


def draw_move_list(key, part):
    segment, moves = make_plan(key)
    return moves


def levels(key, dims, cuts, low, top_value):
    gain = 1.0
    for dim, blocks in cuts:
        steps = jax.random.uniform(jax.random.fold_in(jax.random.fold_in(key, 6), dim), (blocks,), jnp.float32, low / len(cuts), top_value / len(cuts))
        gain = gain * jnp.repeat(jnp.exp(steps), dims[dim] // blocks).reshape((-1,) + (1,) * (len(dims) - 1 - dim))
    return gain


def normal_values(stream_key, dims, scale, bound, cuts=(), held_as=jnp.bfloat16):
    drawn = scale * jax.random.normal(stream_key, dims, jnp.float32)
    if cuts:
        drawn = drawn * levels(stream_key, dims, cuts, -0.22, 0.18)
    return jnp.clip(drawn, -bound, bound).astype(held_as)


def setup_inputs(seed: int = 0) -> dict:
    streams_of = jax.random.split(jax.random.key(seed), 7)
    return {
        "activations": normal_values(streams_of[0], (LAYERS, TOKENS, D), 1.0, 6.0, ((0, 4), (1, 32))),
        "output_grads": normal_values(streams_of[1], (LAYERS, TOKENS, D), 1.0, 6.0, ((0, 4), (1, 32))),
        "in_projection": normal_values(streams_of[2], (LAYERS, KIN, D), D ** -0.5, 0.0625, ((0, 4),)),
        "out_projection": normal_values(streams_of[3], (LAYERS, KOUT, D), D ** -0.5, 0.0625, ((0, 4),)),
        "segment_ids": draw_segment_ids(jax.random.fold_in(streams_of[6], 71), 0),
        "move_list": draw_move_list(jax.random.fold_in(streams_of[6], 71), 0),
    }


DAMPING = 0.05

def layer_terms(acts_layer, grads_layer, proj_in, proj_out, segment_ids, move_list):
    width = KIN * KOUT
    left = jnp.dot(acts_layer.astype(jnp.float32), proj_in.T.astype(jnp.float32), preferred_element_type=jnp.float32).astype(jnp.bfloat16)
    right = jnp.dot(grads_layer.astype(jnp.float32), proj_out.T.astype(jnp.float32), preferred_element_type=jnp.float32).astype(jnp.bfloat16)
    outer = (left.astype(jnp.float32)[:, :, None] * right.astype(jnp.float32)[:, None, :]).reshape(TOKENS, width)
    positions = jnp.arange(TOKENS, dtype=jnp.int32) % TOK_DEV
    previous = jnp.concatenate([segment_ids[:1], segment_ids[:-1]])
    starts = (segment_ids >= 0) & ((positions == 0) | (segment_ids != previous))
    doc_index = jnp.cumsum(starts.astype(jnp.int32)) - 1
    sums = jax.ops.segment_sum(outer, doc_index, num_segments=DOCS)
    lengths = jax.ops.segment_sum(jnp.ones((TOKENS,), jnp.float32), doc_index, num_segments=DOCS)
    doc_features = (sums / jnp.sqrt(lengths)[:, None]).astype(jnp.bfloat16)
    valid = move_list >= 0
    entry_doc = jnp.cumsum(valid.astype(jnp.int32)) - 1
    target = jnp.where(valid, move_list, DOCS).astype(jnp.int32)
    source = jnp.clip(entry_doc, 0, DOCS - 1).astype(jnp.int32)
    placed = jnp.zeros((DOCS, width), jnp.bfloat16).at[target].set(doc_features[source], mode='drop')
    gram = lax.dot_general(placed.astype(jnp.float32), placed.astype(jnp.float32), (((0,), (0,)), ((), ())), preferred_element_type=jnp.float32)
    hessian = gram / DOCS + DAMPING * jnp.eye(width, dtype=jnp.float32)
    lower = jnp.linalg.cholesky(hessian)
    solved = lax.linalg.triangular_solve(lower, placed.T.astype(jnp.float32), left_side=True, lower=True)
    quad = lax.optimization_barrier(jnp.sum(solved * solved, axis=0)) / width
    return (lower.T, placed, quad)

def reference(activations, output_grads, in_projection, out_projection, segment_ids, move_list):
    factors = []
    placed_all = []
    influence = jnp.zeros((DOCS,), jnp.float32)
    for layer_id in range(LAYERS):
        upper, placed, quad = layer_terms(activations[layer_id], output_grads[layer_id], in_projection[layer_id], out_projection[layer_id], segment_ids, move_list)
        factors.append(upper)
        placed_all.append(placed)
        influence = influence + quad
    return (jnp.stack(factors), jnp.stack(placed_all), influence)
```

```python
import functools

import jax
import jax.numpy as jnp
from jax import lax
from jax.experimental import pallas as pl
from jax.experimental.pallas import tpu as pltpu
from jax.sharding import PartitionSpec as P

BAL = 32
B = 128
S = 32
DAMPING = 0.05
F32=jnp.float32; BF=jnp.bfloat16

def split(x):
    hi = x.astype(BF)
    lo = (x - hi.astype(F32)).astype(BF)
    return hi, lo

def dotT(a, b):
    return lax.dot_general(a, b, (((0,),(0,)),((),())), preferred_element_type=F32)
def dot(a, b):
    return lax.dot_general(a, b, (((1,),(0,)),((),())), preferred_element_type=F32)

def chol_rows(D, V, W):
    nb = S//8
    row = lax.broadcasted_iota(jnp.int32,(8,128),0)
    C = [[None]*nb for _ in range(S)]
    for j in range(S):
        for i in range(j//8, nb):
            C[j][i] = jnp.broadcast_to(D[8*i:8*i+8, j:j+1], (8,128))
    Vr = [[V[8*i:8*i+8, 128*c:128*c+128] for c in range(W//128)] for i in range(nb)]
    dv = [jnp.ones((8,128),F32) for _ in range(nb)]
    for j in range(S):
        jb, js = divmod(j,8)
        u = C[j]
        piv = jnp.broadcast_to(u[jb][js:js+1], (8,128))
        r = 1.0/piv
        dv[jb] = jnp.where(row==js, piv, dv[jb])
        w = [None]*nb
        for i in range(jb, nb): w[i] = u[i]*r
        for j2 in range(j+1, S):
            q = jnp.broadcast_to(u[j2//8][j2%8:j2%8+1], (8,128))
            for i in range(j2//8, nb):
                C[j2][i] = C[j2][i] - w[i]*q
        for c in range(W//128):
            vrow = jnp.broadcast_to(Vr[jb][c][js:js+1], (8,128))
            for i in range(jb, nb):
                if i==jb:
                    if js==7: continue
                    wi = jnp.where(row>js, w[i], 0.0)
                else: wi = w[i]
                Vr[i][c] = Vr[i][c] - wi*vrow
    out=[]
    for i in range(nb):
        s = lax.rsqrt(dv[i])
        out.append(jnp.concatenate([Vr[i][c]*s for c in range(W//128)], axis=1))
    return jnp.concatenate(out, axis=0)

def factor_diag(A):
    r_ = lax.broadcasted_iota(jnp.int32,(B,B),0); c_=lax.broadcasted_iota(jnp.int32,(B,B),1)
    eye = jnp.where(r_==c_, 1.0, 0.0).astype(F32)
    V = jnp.concatenate([A, eye], axis=1)
    rows=[]
    for s in range(B//S):
        P = chol_rows(V[:S, s*S:s*S+S], V[:S], 2*B)
        rows.append(P)
        if s < B//S-1:
            h,l = split(P)
            K = jnp.concatenate([h,h,l],axis=0)[:, (s+1)*S:B]
            Q = jnp.concatenate([h,l,h],axis=0)
            V = V[S:] - dotT(K,Q)
    Z = jnp.concatenate(rows,axis=0)
    return Z[:, :B], Z[:, B:]

def k3_kernel(n, f_ref, mine_ref, fac_ref, q_ref, rh, rl):
    docs = f_ref.shape[0]
    W = n + 128
    nb = n//B
    ri = lax.broadcasted_iota(jnp.int32,(B,B),0); ci=lax.broadcasted_iota(jnp.int32,(B,B),1)
    acc = jnp.zeros((1,128),F32)
    for k in range(nb):
        c0 = k*B
        fk = f_ref[:, c0:c0+B]
        H = dotT(fk, f_ref[:, c0:n])*(1.0/docs)
        mk = mine_ref[:, c0:c0+B].astype(F32).T
        X = jnp.concatenate([mk, jnp.zeros((B,128-mk.shape[1]),F32)],axis=1)
        Srow = jnp.concatenate([H, X],axis=1)
        if k>0:
            lh = rh[:c0, c0:c0+B]; ll = rl[:c0, c0:c0+B]
            gh = rh[:c0, c0:W]; gl = rl[:c0, c0:W]
            Srow = Srow - (dotT(lh, gh) + dotT(lh, gl) + dotT(ll, gh))
        A = Srow[:, :B] + jnp.where(ri==ci, DAMPING, 0.0)
        R, T = factor_diag(A)
        R = jnp.where(ci>=ri, R, 0.0)
        th, tl = split(T)
        sh, sl = split(Srow[:, B:])
        Pn = dot(th, sh) + dot(th, sl) + dot(tl, sh)
        fac_ref[c0:c0+B, c0:c0+B] = R
        if k < nb-1:
            fac_ref[c0:c0+B, c0+B:n] = Pn[:, :n-c0-B]
            ph, pl_ = split(Pn)
            rh[c0:c0+B, c0+B:W] = ph
            rl[c0:c0+B, c0+B:W] = pl_
        if k>0:
            fac_ref[c0:c0+B, 0:c0] = jnp.zeros((B,c0),F32)
        sol = Pn[:, n-c0-B:]
        acc = acc + jnp.sum(sol*sol, axis=0, keepdims=True)
    q_ref[...] = jnp.broadcast_to(acc, (8,128))

def k3(f, mine):
    docs, n = f.shape
    return pl.pallas_call(
        functools.partial(k3_kernel, n),
        out_shape=(jax.ShapeDtypeStruct((n,n),F32), jax.ShapeDtypeStruct((8,128),F32)),
        in_specs=[pl.BlockSpec(memory_space=pltpu.VMEM)]*2,
        out_specs=(pl.BlockSpec(memory_space=pltpu.VMEM),)*2,
        scratch_shapes=[pltpu.VMEM((n,n+128),BF), pltpu.VMEM((n,n+128),BF)],
        compiler_params=pltpu.CompilerParams(vmem_limit_bytes=48*2**20),
    )(f, mine)


def shifted(block, axis, distance):
    devices = range(lax.axis_size(axis))
    route = [(i - distance, i) for i in devices if i - distance in devices]
    return lax.ppermute(block, axis, route)


def on_device(activations, output_grads, in_projection, out_projection, segment_ids, move_list):
    contract = (((1,), (1,)), ((), ()))
    left = lax.dot_general(
        in_projection[0], activations[0], contract, preferred_element_type=jnp.float32
    ).astype(jnp.bfloat16)
    right = lax.dot_general(
        out_projection[0], output_grads[0], contract, preferred_element_type=jnp.float32
    ).astype(jnp.bfloat16)
    doc_slots = move_list.shape[0]
    width = left.shape[0] * right.shape[0]
    slot_ids = jnp.arange(doc_slots + 1, dtype=jnp.int32) - 1
    member = (segment_ids[None, :] == slot_ids[:, None]).astype(jnp.bfloat16)
    masked = member[:, None, :] * left[None, :, :]
    blocks = lax.dot_general(
        masked, right, (((2,), (1,)), ((), ())), preferred_element_type=jnp.float32
    )
    sums = blocks.reshape(doc_slots + 1, width)
    counts = jnp.sum(member.astype(jnp.float32), axis=1)
    carried_sum, carried_count = shifted((sums[:1], counts[:1]), "rep", -1)
    last_slot = jnp.max(segment_ids)
    takes = (slot_ids[1:] == last_slot).astype(jnp.float32)
    totals = sums[1:] + takes[:, None] * carried_sum
    lengths = counts[1:] + takes * carried_count[0]
    safe_len = jnp.maximum(lengths, 1.0)
    local_features = (totals / jnp.sqrt(safe_len)[:, None]).astype(jnp.bfloat16)
    replica = lax.axis_index("rep")
    n_rep = lax.axis_size("rep")
    offsets = jnp.where(move_list >= 0, move_list // BAL - replica, 5)
    within = move_list % BAL
    row_ids = jnp.arange(BAL, dtype=jnp.int32)

    def arrange(step_offset):
        select = ((offsets[None, :] == step_offset) & (within[None, :] == row_ids[:, None])).astype(
            jnp.bfloat16
        )
        return jnp.dot(select, local_features, preferred_element_type=jnp.float32).astype(
            jnp.bfloat16
        )

    staying = arrange(0)
    from_right = shifted(arrange(-1), "rep", -1)
    from_left = shifted(arrange(1), "rep", 1)
    mine = (
        staying.astype(jnp.float32) + from_right.astype(jnp.float32) + from_left.astype(jnp.float32)
    ).astype(jnp.bfloat16)
    everyone = lax.all_gather(mine, "rep", axis=0, tiled=True)
    factor, quad = k3(everyone, mine)
    quad = quad[0, :BAL] / width
    influence = lax.psum(quad, "layer")
    return (factor[None], mine[None], influence)


def solution(mesh):
    placed = (
        P("layer", "rep", None),
        P("layer", "rep", None),
        P("layer", None, None),
        P("layer", None, None),
        P("rep"),
        P("rep"),
    )
    return jax.shard_map(
        on_device,
        mesh=mesh,
        in_specs=placed,
        out_specs=(P("layer", None, None), P("layer", "rep", None), P("rep")),
        check_vma=False,
    )
```

```python
import functools

import jax
import jax.numpy as jnp
from jax import lax
from jax.experimental import pallas as pl
from jax.experimental.pallas import tpu as pltpu
from jax.sharding import PartitionSpec

BAL = 32
BLOCK = 128
GROUP = 32
DAMPING = 0.05
TOK = 128
F32 = jnp.float32
BF16 = jnp.bfloat16
VMEM = pl.BlockSpec(memory_space=pltpu.VMEM)


def split(x):
    hi = x.astype(BF16)
    lo = (x - hi.astype(F32)).astype(BF16)
    return hi, lo


def dot_t(a, b):
    return lax.dot_general(a, b, (((0,), (0,)), ((), ())), preferred_element_type=F32)


def dot(a, b):
    return lax.dot_general(a, b, (((1,), (0,)), ((), ())), preferred_element_type=F32)


def iota(shape, axis):
    return lax.broadcasted_iota(jnp.int32, shape, axis)


def onehot(mask, dtype=BF16):
    return jnp.where(mask, 1.0, 0.0).astype(dtype)


def front_kernel(
    steps_k, acts_ref, grads_ref, in_ref, out_ref, segs_ref, moves_ref,
    arr_ref, aux_ref, left_acc, right_acc, sums, counts, moves_pad,
):
    step, part = pl.program_id(0), pl.program_id(1)
    replica = lax.axis_index("rep")
    kin, kout = left_acc.shape[1], right_acc.shape[1]
    slots, width = sums.shape
    doc_slots = moves_ref.shape[1]
    contract = (((1,), (1,)), ((), ()))
    left_part = lax.dot_general(acts_ref[...], in_ref[...], contract, preferred_element_type=F32)
    right_part = lax.dot_general(grads_ref[...], out_ref[...], contract, preferred_element_type=F32)

    @pl.when(part == 0)
    def _():
        left_acc[...] = left_part
        right_acc[...] = right_part

    @pl.when(part > 0)
    def _():
        left_acc[...] += left_part
        right_acc[...] += right_part

    @pl.when((step == 0) & (part == 0))
    def _():
        sums[...] = jnp.zeros_like(sums)
        counts[...] = jnp.zeros_like(counts)
        moves_pad[...] = jnp.full_like(moves_pad, -1)
        moves_pad[:, :doc_slots] = moves_ref[...]

    @pl.when(part == steps_k - 1)
    def _():
        left = left_acc[...].astype(BF16)
        right = right_acc[...].astype(BF16)
        lane, sub = iota((kin, width), 1), iota((kin, width), 0)
        spread = onehot(lane // kout == sub)
        lane, sub = iota((kout, width), 1), iota((kout, width), 0)
        repeat = onehot(lane % kout == sub)
        hi, lo = split(dot(left, spread) * dot(right, repeat))
        here = segs_ref[:, pl.ds(pl.multiple_of(step * TOK, TOK), TOK)]
        slot = iota((slots, TOK), 0)
        slot = jnp.where(slot == doc_slots, -1, slot)
        member = onehot(slot == here, F32)
        member_low = member.astype(BF16)
        sums[...] += dot(member_low, hi) + dot(member_low, lo)
        counts[...] += jnp.broadcast_to(jnp.sum(member, axis=1, keepdims=True), counts.shape)

    @pl.when((step == pl.num_programs(0) - 1) & (part == steps_k - 1))
    def _():
        total, count = sums[...], counts[...]
        moves = moves_pad[...]
        last = jnp.max(segs_ref[...], axis=1, keepdims=True)
        lanes = moves.shape[1]
        scale = 1.0 / jnp.sqrt(jnp.maximum(count, 1.0))
        scale = jnp.concatenate([scale] * (width // scale.shape[1]), axis=1)
        local = (total * scale).astype(BF16)
        local = jnp.concatenate([local, jnp.zeros((lanes - slots, width), BF16)], axis=0)
        row, slot = iota((3 * BAL, lanes), 0), iota((3 * BAL, lanes), 1)
        offset = jnp.where(row < BAL, 0, jnp.where(row < 2 * BAL, -1, 1))
        target = (replica + offset) * BAL + row % BAL
        chosen = (moves == target) & (moves >= 0) & (slot != last)
        arr_ref[...] = dot(onehot(chosen), local).astype(BF16)
        is_last = iota((slots, width), 0) == last
        last_sum = jnp.sum(jnp.where(is_last, total, 0.0), axis=0, keepdims=True)
        is_last = iota(counts.shape, 0) == last
        last_count = jnp.sum(jnp.where(is_last, count, 0.0), axis=0, keepdims=True)
        goes_to = jnp.sum(jnp.where(iota(moves.shape, 1) == last, moves, 0), axis=1, keepdims=True)
        row = iota((8, width), 0)
        wide = [last_sum, total[doc_slots : doc_slots + 1]]
        wide += [jnp.broadcast_to(v[:, :1], (1, width)) for v in (last_count, count[doc_slots : doc_slots + 1])]
        wide += [jnp.broadcast_to(goes_to.astype(F32), (1, width))]
        aux = jnp.zeros((8, width), F32)
        for i, v in enumerate(wide):
            aux = jnp.where(row == i, v, aux)
        aux_ref[...] = aux


def front(acts, grads, in_proj, out_proj, segs, moves, steps_k=2):
    tokens, depth = acts.shape
    kin, kout = in_proj.shape[0], out_proj.shape[0]
    width = kin * kout
    cut = depth // steps_k
    slots = -(-(moves.shape[1] + 1) // 16) * 16
    whole = lambda i, k: (0, 0)
    return pl.pallas_call(
        functools.partial(front_kernel, steps_k),
        grid=(tokens // TOK, steps_k),
        in_specs=[
            pl.BlockSpec((TOK, cut), lambda i, k: (i, k)),
            pl.BlockSpec((TOK, cut), lambda i, k: (i, k)),
            pl.BlockSpec((kin, cut), lambda i, k: (0, k)),
            pl.BlockSpec((kout, cut), lambda i, k: (0, k)),
            pl.BlockSpec(segs.shape, whole),
            pl.BlockSpec(moves.shape, whole),
        ],
        out_specs=(pl.BlockSpec((3 * BAL, width), whole), pl.BlockSpec((8, width), whole)),
        out_shape=(
            jax.ShapeDtypeStruct((3 * BAL, width), BF16),
            jax.ShapeDtypeStruct((8, width), F32),
        ),
        scratch_shapes=[
            pltpu.VMEM((TOK, kin), F32),
            pltpu.VMEM((TOK, kout), F32),
            pltpu.VMEM((slots, width), F32),
            pltpu.VMEM((slots, 128), F32),
            pltpu.VMEM((1, 128), jnp.int32),
        ],
        compiler_params=pltpu.CompilerParams(vmem_limit_bytes=40 * 2**20),
    )(acts, grads, in_proj, out_proj, segs, moves)


def gather_kernel(side, cores, arr_ref, aux_ref, all_ref, from_right, from_left, aux_in, ex_send, ex_recv, send, recv):
    n_rep = side * side * cores
    width = all_ref.shape[1]
    me = lax.axis_index("rep")
    core = me % cores
    spot_z = (me // cores) % side
    spot_x = me // (cores * side)

    def rep_at(dx, dz, c):
        x, z = (spot_x + dx + side) % side, (spot_z + dz + side) % side
        return (x * side + z) * cores + c

    right, left, left2 = (me + 1) % n_rep, (me + n_rep - 1) % n_rep, (me + n_rep - 2) % n_rep
    right2 = (me + 2) % n_rep
    sibling = rep_at(0, 0, 1 - core)
    around = [rep_at(1, 0, core), rep_at(-1, 0, core), rep_at(0, 1, core), rep_at(0, -1, core)]
    barrier = pltpu.get_barrier_semaphore()
    senders = [right, left, right2, sibling] + around
    for device in senders:
        pl.semaphore_signal(barrier, inc=1, device_id={"rep": device}, device_id_type=pl.DeviceIdType.MESH)
    pl.semaphore_wait(barrier, len(senders))

    def copy(src, dst, s, r, device):
        return pltpu.make_async_remote_copy(
            src_ref=src, dst_ref=dst, send_sem=s, recv_sem=r,
            device_id={"rep": device}, device_id_type=pl.DeviceIdType.MESH,
        )

    first = [
        copy(aux_ref, aux_in.at[0], ex_send.at[0], ex_recv.at[0], left),
        copy(aux_ref, aux_in.at[1], ex_send.at[1], ex_recv.at[1], right),
        copy(aux_ref, aux_in.at[2], ex_send.at[2], ex_recv.at[2], left2),
        copy(arr_ref.at[pl.ds(BAL, BAL)], from_right, ex_send.at[3], ex_recv.at[3], left),
        copy(arr_ref.at[pl.ds(2 * BAL, BAL)], from_left, ex_send.at[4], ex_recv.at[4], right),
    ]
    for c in first:
        c.start()
    for c in first:
        c.wait_recv()

    mine = arr_ref[pl.ds(0, BAL), :].astype(F32) + from_right[...].astype(F32) + from_left[...].astype(F32)
    own = aux_ref[...]
    after, before, after2 = aux_in[0], aux_in[1], aux_in[2]
    row = iota((BAL, width), 0).astype(F32)
    base = (me * BAL).astype(F32)
    for a, b in ((before, own), (own, after), (after, after2)):
        length = jnp.maximum(a[2:3] + b[3:4], 1.0)
        feature = (a[0:1] + b[1:2]) * (1.0 / jnp.sqrt(length))
        mine = jnp.where(row == a[4:5] - base, feature, mine)
    all_ref[pl.ds(pl.multiple_of(me * BAL, BAL), BAL), :] = mine.astype(BF16)

    half, quarter = width // 2, width // 4
    sent = []

    def piece(dx, dz, c, col, cols):
        start = pl.multiple_of(rep_at(dx, dz, c) * BAL, BAL)
        return all_ref.at[pl.ds(start, BAL), pl.ds(col, cols)]

    def start(index, dx, dz, col, cols, device):
        ref = piece(dx, dz, core, col, cols)
        c = copy(ref, ref, send.at[index], recv.at[index], device)
        c.start()
        sent.append(c)

    def arrived(index, dx, dz, c, col, cols):
        ref = piece(dx, dz, c, col, cols)
        copy(ref, ref, send.at[index], recv.at[index], sibling).wait_recv()

    def place(kind, du, dv):
        return (du, dv) if kind == 0 else (dv, du)

    def to(kind, du, dv):
        return rep_at(*place(kind, du, dv), core)

    order = (0, -1, 1, 2)
    per_kind = 36

    def first_hop(kind):
        col, n = kind * half, kind * per_kind
        start(n + 0, 0, 0, col, half, to(kind, 1, 0))
        start(n + 1, 0, 0, col, half, to(kind, -1, 0))

    def across(kind, d):
        col, n = kind * half, kind * per_kind + 4 + 4 * order.index(d)
        at = place(kind, d, 0)
        start(n + 0, *at, col, half, to(kind, 0, 1))
        start(n + 1, *at, col, half, to(kind, 0, -1))

    def share(kind, du, dv):
        n = kind * per_kind + 20 + 4 * order.index(du) + order.index(dv)
        start(n, *place(kind, du, dv), kind * half, half, sibling)

    def relay(kind, d):
        col, n = kind * half, kind * per_kind + 4 + 4 * order.index(d)
        at = place(kind, d, -1)
        arrived(n + 0, *at, core, col, half)
        start(n + 2, *at, col, quarter, to(kind, 0, 1))
        share(kind, d, -1)
        at = place(kind, d, 1)
        arrived(n + 1, *at, core, col, half)
        start(n + 3, *at, col + quarter, quarter, to(kind, 0, -1))
        share(kind, d, 1)

    def finish(kind, d):
        col, n = kind * half, kind * per_kind + 4 + 4 * order.index(d)
        at = place(kind, d, 2)
        arrived(n + 2, *at, core, col, quarter)
        arrived(n + 3, *at, core, col + quarter, quarter)
        share(kind, d, 2)

    for kind in (0, 1):
        first_hop(kind)
    for kind in (0, 1):
        across(kind, 0)
    for kind in (0, 1):
        share(kind, 0, 0)
    for sign, q in ((-1, 0), (1, 1)):
        for kind in (0, 1):
            col, n = kind * half, kind * per_kind
            at = place(kind, sign, 0)
            arrived(n + q, *at, core, col, half)
            start(n + 2 + q, *at, col + q * quarter, quarter, to(kind, -sign, 0))
            across(kind, sign)
            share(kind, sign, 0)
    for kind in (0, 1):
        relay(kind, 0)
    for kind in (0, 1):
        col, n = kind * half, kind * per_kind
        at = place(kind, 2, 0)
        arrived(n + 2, *at, core, col, quarter)
        arrived(n + 3, *at, core, col + quarter, quarter)
        across(kind, 2)
        share(kind, 2, 0)
    for d in (-1, 1, 2):
        for kind in (0, 1):
            relay(kind, d)
    for d in order:
        for kind in (0, 1):
            finish(kind, d)
    for kind in (0, 1):
        for i, du in enumerate(order):
            for j, dv in enumerate(order):
                n = kind * per_kind + 20 + 4 * i + j
                arrived(n, *place(kind, du, dv), 1 - core, kind * half, half)
    for c in first + sent:
        c.wait_send()


def gather(arr, aux, n_rep):
    width = arr.shape[1]
    cores = 2
    side = round((n_rep // cores) ** 0.5)
    return pl.pallas_call(
        functools.partial(gather_kernel, side, cores),
        out_shape=jax.ShapeDtypeStruct((BAL * n_rep, width), BF16),
        in_specs=[VMEM, VMEM],
        out_specs=VMEM,
        scratch_shapes=[
            pltpu.VMEM((BAL, width), BF16),
            pltpu.VMEM((BAL, width), BF16),
            pltpu.VMEM((3, 8, width), F32),
            pltpu.SemaphoreType.DMA((5,)),
            pltpu.SemaphoreType.DMA((5,)),
            pltpu.SemaphoreType.DMA((72,)),
            pltpu.SemaphoreType.DMA((72,)),
        ],
        compiler_params=pltpu.CompilerParams(
            collective_id=0, has_side_effects=True, vmem_limit_bytes=16 * 2**20
        ),
    )(arr, aux)


def pivot_rows(D, V):
    size, width = V.shape
    tiles, strips = size // 8, width // 128
    row = iota((8, 128), 0)
    cols = [
        [jnp.broadcast_to(D[8 * i : 8 * i + 8, j : j + 1], (8, 128)) if i >= j // 8 else None for i in range(tiles)]
        for j in range(size)
    ]
    rows = [[V[8 * i : 8 * i + 8, 128 * c : 128 * c + 128] for c in range(strips)] for i in range(tiles)]
    pivots = [jnp.ones((8, 128), F32) for _ in range(tiles)]
    for j in range(size):
        tile, sub = divmod(j, 8)
        column = cols[j]
        pivot = jnp.broadcast_to(column[tile][sub : sub + 1], (8, 128))
        inverse = 1.0 / pivot
        pivots[tile] = jnp.where(row == sub, pivot, pivots[tile])
        factor = [column[i] * inverse if i >= tile else None for i in range(tiles)]
        for j2 in range(j + 1, size):
            other = jnp.broadcast_to(column[j2 // 8][j2 % 8 : j2 % 8 + 1], (8, 128))
            for i in range(j2 // 8, tiles):
                cols[j2][i] = cols[j2][i] - factor[i] * other
        for c in range(strips):
            source = jnp.broadcast_to(rows[tile][c][sub : sub + 1], (8, 128))
            for i in range(tile, tiles):
                weight = jnp.where(row > sub, factor[i], 0.0) if i == tile else factor[i]
                rows[i][c] = rows[i][c] - weight * source
    out = []
    for i in range(tiles):
        scale = lax.rsqrt(pivots[i])
        out.append(jnp.concatenate([rows[i][c] * scale for c in range(strips)], axis=1))
    return jnp.concatenate(out, axis=0)


def factor_block(A):
    same = iota((BLOCK, BLOCK), 0) == iota((BLOCK, BLOCK), 1)
    V = jnp.concatenate([A, onehot(same, F32)], axis=1)
    done = []
    for at in range(0, BLOCK, GROUP):
        rows = pivot_rows(V[:GROUP, at : at + GROUP], V[:GROUP])
        done.append(rows)
        if at + GROUP < BLOCK:
            hi, lo = split(rows)
            here = jnp.concatenate([hi, hi, lo], axis=0)[:, at + GROUP : BLOCK]
            V = V[GROUP:] - dot_t(here, jnp.concatenate([hi, lo, hi], axis=0))
    both = jnp.concatenate(done, axis=0)
    return both[:, :BLOCK], both[:, BLOCK:]


def factor_kernel(all_ref, fac_ref, mine_ref, quad_ref, high, low):
    docs, n = all_ref.shape
    width = n + 128
    replica = lax.axis_index("rep")
    mine = all_ref[pl.ds(pl.multiple_of(replica * BAL, BAL), BAL), :]
    mine_ref[...] = mine
    ri, ci = iota((BLOCK, BLOCK), 0), iota((BLOCK, BLOCK), 1)
    quad = jnp.zeros((1, 128), F32)
    for a in range(0, n, BLOCK):
        b = a + BLOCK
        hessian = dot_t(all_ref[:, a:b], all_ref[:, a:n]) * (1.0 / docs)
        extra = mine[:, a:b].astype(F32).T
        extra = jnp.concatenate([extra, jnp.zeros((BLOCK, 128 - BAL), F32)], axis=1)
        panel = jnp.concatenate([hessian, extra], axis=1)
        if a > 0:
            lh, ll = high[:a, a:b], low[:a, a:b]
            gh, gl = high[:a, a:width], low[:a, a:width]
            panel = panel - (dot_t(lh, gh) + dot_t(lh, gl) + dot_t(ll, gh))
        upper, inverse = factor_block(panel[:, :BLOCK] + jnp.where(ri == ci, DAMPING, 0.0))
        fac_ref[a:b, a:b] = jnp.where(ci >= ri, upper, 0.0)
        th, tl = split(inverse)
        sh, sl = split(panel[:, BLOCK:])
        solved = dot(th, sh) + dot(th, sl) + dot(tl, sh)
        if b < n:
            fac_ref[a:b, b:n] = solved[:, : n - b]
            hi, lo = split(solved)
            high[a:b, b:width] = hi
            low[a:b, b:width] = lo
        if a > 0:
            fac_ref[a:b, :a] = jnp.zeros((BLOCK, a), F32)
        tail = solved[:, n - b :]
        quad = quad + jnp.sum(tail * tail, axis=0, keepdims=True)
    quad_ref[...] = jnp.broadcast_to(quad * (1.0 / n), quad_ref.shape)


def factor(everyone):
    docs, n = everyone.shape
    return pl.pallas_call(
        factor_kernel,
        out_shape=(
            jax.ShapeDtypeStruct((n, n), F32),
            jax.ShapeDtypeStruct((BAL, n), BF16),
            jax.ShapeDtypeStruct((8, 128), F32),
        ),
        in_specs=[VMEM],
        out_specs=(VMEM, VMEM, VMEM),
        scratch_shapes=[pltpu.VMEM((n, n + 128), BF16), pltpu.VMEM((n, n + 128), BF16)],
        compiler_params=pltpu.CompilerParams(vmem_limit_bytes=40 * 2**20),
    )(everyone)


def layer_sum_kernel(layers, quad_ref, out_ref, inbox, send, recv):
    me = lax.axis_index("layer")
    barrier = pltpu.get_barrier_semaphore()
    for step in range(1, layers):
        device = (me + step) % layers
        pl.semaphore_signal(barrier, inc=1, device_id={"layer": device}, device_id_type=pl.DeviceIdType.MESH)
    pl.semaphore_wait(barrier, layers - 1)
    copies = []
    for step in range(1, layers):
        copies.append(
            pltpu.make_async_remote_copy(
                src_ref=quad_ref, dst_ref=inbox.at[step - 1], send_sem=send.at[step - 1],
                recv_sem=recv.at[step - 1], device_id={"layer": (me + step) % layers},
                device_id_type=pl.DeviceIdType.MESH,
            )
        )
        copies[-1].start()
    total = quad_ref[...]
    for step, c in enumerate(copies):
        c.wait_recv()
        total = total + inbox[step]
    out_ref[...] = total[:1, :BAL]
    for c in copies:
        c.wait_send()


def layer_sum(quad, layers):
    return pl.pallas_call(
        functools.partial(layer_sum_kernel, layers),
        out_shape=jax.ShapeDtypeStruct((1, BAL), F32),
        in_specs=[VMEM],
        out_specs=VMEM,
        scratch_shapes=[
            pltpu.VMEM((layers - 1,) + quad.shape, F32),
            pltpu.SemaphoreType.DMA((layers - 1,)),
            pltpu.SemaphoreType.DMA((layers - 1,)),
        ],
        compiler_params=pltpu.CompilerParams(collective_id=1, has_side_effects=True),
    )(quad)


def on_device(n_rep, layers, activations, output_grads, in_projection, out_projection, segment_ids, move_list):
    arranged, aux = front(
        activations[0], output_grads[0], in_projection[0], out_projection[0],
        segment_ids[None], move_list[None],
    )
    everyone = gather(arranged, aux, n_rep)
    upper, mine, quad = factor(everyone)
    influence = layer_sum(quad, layers)
    return (upper[None], mine[None], influence[0])


def solution(mesh):
    placed = (
        PartitionSpec("layer", "rep", None),
        PartitionSpec("layer", "rep", None),
        PartitionSpec("layer", None, None),
        PartitionSpec("layer", None, None),
        PartitionSpec("rep"),
        PartitionSpec("rep"),
    )
    return jax.shard_map(
        functools.partial(on_device, mesh.shape["rep"], mesh.shape["layer"]),
        mesh=mesh,
        in_specs=placed,
        out_specs=(PartitionSpec("layer", None, None), PartitionSpec("layer", "rep", None), PartitionSpec("rep")),
        check_vma=False,
    )
```

```python
import functools

import jax
import jax.numpy as jnp
from jax import lax
from jax.experimental import pallas as pl
from jax.experimental.pallas import tpu as pltpu
from jax.sharding import PartitionSpec

BAL = 32
BLOCK = 128
GROUP = 32
DAMPING = 0.05
F32 = jnp.float32
BF16 = jnp.bfloat16
VMEM = pl.BlockSpec(memory_space=pltpu.VMEM)


def split(x):
    hi = x.astype(BF16)
    lo = (x - hi.astype(F32)).astype(BF16)
    return hi, lo


def dot_t(a, b):
    return lax.dot_general(a, b, (((0,), (0,)), ((), ())), preferred_element_type=F32)


def dot(a, b):
    return lax.dot_general(a, b, (((1,), (0,)), ((), ())), preferred_element_type=F32)


def iota(shape, axis):
    return lax.broadcasted_iota(jnp.int32, shape, axis)


def onehot(mask, dtype=BF16):
    return jnp.where(mask, 1.0, 0.0).astype(dtype)

CHUNKS = (64, 128, 128, 128, 64)
AHEAD = 2


def project(block, proj):
    contract = (((1,), (1,)), ((), ()))
    return lax.dot_general(block, proj, contract, preferred_element_type=F32).astype(BF16)


def expand(x, pattern):
    return dot(x, pattern)


def front_kernel(
    acts_hbm, grads_hbm, in_hbm, out_hbm, segs_hbm, moves_hbm, arr_ref, aux_ref,
    acts, grads, in_proj, out_proj, segs, moves_in, sums, counts, moves_pad, sem, small_sem,
):
    replica = lax.axis_index("rep")
    kin, kout = in_proj.shape[0], out_proj.shape[0]
    slots, width = sums.shape
    doc_slots = moves_in.shape[1]
    small = [
        pltpu.make_async_copy(a, b, small_sem.at[i])
        for i, (a, b) in enumerate(
            ((in_hbm, in_proj), (out_hbm, out_proj), (segs_hbm, segs), (moves_hbm, moves_in))
        )
    ]
    large = []
    ends = [sum(CHUNKS[: c + 1]) for c in range(len(CHUNKS))]
    for c, size in enumerate(CHUNKS):
        rows = pl.ds(ends[c] - size, size)
        large.append(
            (
                pltpu.make_async_copy(acts_hbm.at[rows], acts.at[rows], sem.at[0, c]),
                pltpu.make_async_copy(grads_hbm.at[rows], grads.at[rows], sem.at[1, c]),
            )
        )
    small[0].start()
    small[1].start()
    for pair in large[:AHEAD]:
        pair[0].start()
        pair[1].start()
    small[2].start()
    small[3].start()
    lane, sub = iota((kin, width), 1), iota((kin, width), 0)
    spread = onehot(lane // kout == sub)
    lane, sub = iota((kout, width), 1), iota((kout, width), 0)
    repeat = onehot(lane % kout == sub)
    moves_pad[...] = jnp.full_like(moves_pad, -1)
    def gather_documents(c, left, right):
        hi, lo = split(expand(left, spread) * expand(right, repeat))
        size = CHUNKS[c]
        here = segs[:, ends[c] - size : ends[c]]
        slot = iota((slots, size), 0)
        slot = jnp.where(slot == doc_slots, -1, slot)
        member = onehot(slot == here, F32)
        member_low = member.astype(BF16)
        part = dot(member_low, hi) + dot(member_low, lo)
        number = jnp.broadcast_to(jnp.sum(member, axis=1, keepdims=True), counts.shape)
        if c == 0:
            sums[...] = part
            counts[...] = number
        else:
            sums[...] += part
            counts[...] += number

    held = None
    for copy in small:
        copy.wait()
    for c, size in enumerate(CHUNKS):
        rows = pl.ds(ends[c] - size, size)
        for copy in large[c]:
            copy.wait()
        if c + AHEAD < len(CHUNKS):
            for copy in large[c + AHEAD]:
                copy.start()
        left = project(acts[rows, :], in_proj[...])
        right = project(grads[rows, :], out_proj[...])
        if c > 0:
            gather_documents(c - 1, *held)
        held = left, right
    gather_documents(len(CHUNKS) - 1, *held)
    moves_pad[:, :doc_slots] = moves_in[...]
    total, count = sums[...], counts[...]
    moves = moves_pad[...]
    last = jnp.max(segs[...], axis=1, keepdims=True)
    lanes = moves.shape[1]
    scale = 1.0 / jnp.sqrt(jnp.maximum(count, 1.0))
    scale = jnp.concatenate([scale] * (width // scale.shape[1]), axis=1)
    local = (total * scale).astype(BF16)
    local = jnp.concatenate([local, jnp.zeros((lanes - slots, width), BF16)], axis=0)
    row, slot = iota((3 * BAL, lanes), 0), iota((3 * BAL, lanes), 1)
    offset = jnp.where(row < BAL, 0, jnp.where(row < 2 * BAL, -1, 1))
    target = (replica + offset) * BAL + row % BAL
    chosen = (moves == target) & (moves >= 0) & (slot != last)
    arr_ref[...] = dot(onehot(chosen), local).astype(BF16)
    is_last = iota((slots, width), 0) == last
    last_sum = jnp.sum(jnp.where(is_last, total, 0.0), axis=0, keepdims=True)
    is_last = iota(counts.shape, 0) == last
    last_count = jnp.sum(jnp.where(is_last, count, 0.0), axis=0, keepdims=True)
    goes_to = jnp.sum(jnp.where(iota(moves.shape, 1) == last, moves, 0), axis=1, keepdims=True)
    row = iota((8, width), 0)
    wide = [last_sum, total[doc_slots : doc_slots + 1]]
    wide += [jnp.broadcast_to(v[:, :1], (1, width)) for v in (last_count, count[doc_slots : doc_slots + 1])]
    wide += [jnp.broadcast_to(goes_to.astype(F32), (1, width))]
    aux = jnp.zeros((8, width), F32)
    for i, v in enumerate(wide):
        aux = jnp.where(row == i, v, aux)
    aux_ref[...] = aux


def front(acts, grads, in_proj, out_proj, segs, moves):
    tokens, depth = acts.shape
    kin, kout = in_proj.shape[0], out_proj.shape[0]
    width = kin * kout
    slots = -(-(moves.shape[1] + 1) // 16) * 16
    acts, grads, in_proj, out_proj, segs, moves = (
        pltpu.with_memory_space_constraint(v, pltpu.HBM) for v in (acts, grads, in_proj, out_proj, segs, moves)
    )
    held = pl.BlockSpec(memory_space=pltpu.HBM)
    return pl.pallas_call(
        front_kernel,
        in_specs=[held] * 6,
        out_specs=(VMEM, VMEM),
        out_shape=(
            jax.ShapeDtypeStruct((3 * BAL, width), BF16),
            jax.ShapeDtypeStruct((8, width), F32),
        ),
        scratch_shapes=[
            pltpu.VMEM(acts.shape, BF16),
            pltpu.VMEM(grads.shape, BF16),
            pltpu.VMEM(in_proj.shape, BF16),
            pltpu.VMEM(out_proj.shape, BF16),
            pltpu.VMEM(segs.shape, jnp.int32),
            pltpu.VMEM(moves.shape, jnp.int32),
            pltpu.VMEM((slots, width), F32),
            pltpu.VMEM((slots, 128), F32),
            pltpu.VMEM((1, 128), jnp.int32),
            pltpu.SemaphoreType.DMA((2, len(CHUNKS))),
            pltpu.SemaphoreType.DMA((4,)),
        ],
        compiler_params=pltpu.CompilerParams(vmem_limit_bytes=40 * 2**20),
    )(acts, grads, in_proj, out_proj, segs, moves)


def gather_kernel(side, cores, arr_ref, aux_ref, all_ref, from_right, from_left, aux_in, ex_send, ex_recv, send, recv):
    n_rep = side * side * cores
    width = all_ref.shape[1]
    me = lax.axis_index("rep")
    core = me % cores
    spot_z = (me // cores) % side
    spot_x = me // (cores * side)

    def rep_at(dx, dz, c):
        x, z = (spot_x + dx + side) % side, (spot_z + dz + side) % side
        return (x * side + z) * cores + c

    right, left, left2 = (me + 1) % n_rep, (me + n_rep - 1) % n_rep, (me + n_rep - 2) % n_rep
    right2 = (me + 2) % n_rep
    sibling = rep_at(0, 0, 1 - core)
    around = [rep_at(d, 0, core) for d in (1, -1, 2)] + [rep_at(0, d, core) for d in (1, -1, 2)]
    barrier = pltpu.get_barrier_semaphore()
    senders = [right, left, right2, sibling] + around
    for device in senders:
        pl.semaphore_signal(barrier, inc=1, device_id={"rep": device}, device_id_type=pl.DeviceIdType.MESH)
    pl.semaphore_wait(barrier, len(senders))

    def copy(src, dst, s, r, device):
        return pltpu.make_async_remote_copy(
            src_ref=src, dst_ref=dst, send_sem=s, recv_sem=r,
            device_id={"rep": device}, device_id_type=pl.DeviceIdType.MESH,
        )

    first = [
        copy(aux_ref, aux_in.at[0], ex_send.at[0], ex_recv.at[0], left),
        copy(aux_ref, aux_in.at[1], ex_send.at[1], ex_recv.at[1], right),
        copy(aux_ref, aux_in.at[2], ex_send.at[2], ex_recv.at[2], left2),
        copy(arr_ref.at[pl.ds(BAL, BAL)], from_right, ex_send.at[3], ex_recv.at[3], left),
        copy(arr_ref.at[pl.ds(2 * BAL, BAL)], from_left, ex_send.at[4], ex_recv.at[4], right),
    ]
    for c in first:
        c.start()
    for c in first:
        c.wait_recv()

    mine = arr_ref[pl.ds(0, BAL), :].astype(F32) + from_right[...].astype(F32) + from_left[...].astype(F32)
    own = aux_ref[...]
    after, before, after2 = aux_in[0], aux_in[1], aux_in[2]
    row = iota((BAL, width), 0).astype(F32)
    base = (me * BAL).astype(F32)
    for a, b in ((before, own), (own, after), (after, after2)):
        length = jnp.maximum(a[2:3] + b[3:4], 1.0)
        feature = (a[0:1] + b[1:2]) * (1.0 / jnp.sqrt(length))
        mine = jnp.where(row == a[4:5] - base, feature, mine)
    all_ref[pl.ds(pl.multiple_of(me * BAL, BAL), BAL), :] = mine.astype(BF16)

    half = width // 2
    sent = []

    def piece(dx, dz, c, col, cols):
        start = pl.multiple_of(rep_at(dx, dz, c) * BAL, BAL)
        return all_ref.at[pl.ds(start, BAL), pl.ds(col, cols)]

    def start(index, dx, dz, col, cols, device):
        ref = piece(dx, dz, core, col, cols)
        c = copy(ref, ref, send.at[index], recv.at[index], device)
        c.start()
        sent.append(c)

    def arrived(index, dx, dz, c, col, cols):
        ref = piece(dx, dz, c, col, cols)
        copy(ref, ref, send.at[index], recv.at[index], sibling).wait_recv()

    def place(kind, du, dv):
        return (du, dv) if kind == 0 else (dv, du)

    def to(kind, du, dv):
        return rep_at(*place(kind, du, dv), core)

    order = (0, 1, -1, 2)
    per_kind = 3 + 12 + 16

    def along(kind):
        for i, d in enumerate(order[1:]):
            start(kind * per_kind + i, 0, 0, kind * half, half, to(kind, d, 0))

    def across(kind, du):
        at = place(kind, du, 0)
        for i, d in enumerate(order[1:]):
            n = kind * per_kind + 3 + 3 * order.index(du) + i
            start(n, *at, kind * half, half, to(kind, 0, d))

    def share(kind, du, dv):
        n = kind * per_kind + 15 + 4 * order.index(du) + order.index(dv)
        start(n, *place(kind, du, dv), kind * half, half, sibling)

    def back(d):
        return d if d == 2 else -d

    for kind in (0, 1):
        along(kind)
    for kind in (0, 1):
        across(kind, 0)
        share(kind, 0, 0)
    for i, d in enumerate(order[1:]):
        for kind in (0, 1):
            arrived(kind * per_kind + i, *place(kind, back(d), 0), core, kind * half, half)
            across(kind, back(d))
            share(kind, back(d), 0)
    for du in (0, -1, 1, 2):
        for i, d in enumerate(order[1:]):
            for kind in (0, 1):
                n = kind * per_kind + 3 + 3 * order.index(du) + i
                arrived(n, *place(kind, du, back(d)), core, kind * half, half)
                share(kind, du, back(d))
    for kind in (0, 1):
        for i, du in enumerate(order):
            for j, dv in enumerate(order):
                n = kind * per_kind + 15 + 4 * i + j
                arrived(n, *place(kind, du, dv), 1 - core, kind * half, half)
    for c in first + sent:
        c.wait_send()


def gather(arr, aux, n_rep):
    width = arr.shape[1]
    cores = 2
    side = round((n_rep // cores) ** 0.5)
    return pl.pallas_call(
        functools.partial(gather_kernel, side, cores),
        out_shape=jax.ShapeDtypeStruct((BAL * n_rep, width), BF16),
        in_specs=[VMEM, VMEM],
        out_specs=VMEM,
        scratch_shapes=[
            pltpu.VMEM((BAL, width), BF16),
            pltpu.VMEM((BAL, width), BF16),
            pltpu.VMEM((3, 8, width), F32),
            pltpu.SemaphoreType.DMA((5,)),
            pltpu.SemaphoreType.DMA((5,)),
            pltpu.SemaphoreType.DMA((62,)),
            pltpu.SemaphoreType.DMA((62,)),
        ],
        compiler_params=pltpu.CompilerParams(
            collective_id=0, has_side_effects=True, vmem_limit_bytes=16 * 2**20
        ),
    )(arr, aux)


def pivot_rows(D, V):
    size, width = V.shape
    tiles, strips = size // 8, width // 128
    row = iota((8, 128), 0)
    cols = [
        [jnp.broadcast_to(D[8 * i : 8 * i + 8, j : j + 1], (8, 128)) if i >= j // 8 else None for i in range(tiles)]
        for j in range(size)
    ]
    rows = [[V[8 * i : 8 * i + 8, 128 * c : 128 * c + 128] for c in range(strips)] for i in range(tiles)]
    pivots = [jnp.ones((8, 128), F32) for _ in range(tiles)]
    for j in range(size):
        tile, sub = divmod(j, 8)
        column = cols[j]
        pivot = jnp.broadcast_to(column[tile][sub : sub + 1], (8, 128))
        inverse = 1.0 / pivot
        pivots[tile] = jnp.where(row == sub, pivot, pivots[tile])
        factor = [column[i] * inverse if i >= tile else None for i in range(tiles)]
        for j2 in range(j + 1, size):
            other = jnp.broadcast_to(column[j2 // 8][j2 % 8 : j2 % 8 + 1], (8, 128))
            for i in range(j2 // 8, tiles):
                cols[j2][i] = cols[j2][i] - factor[i] * other
        for c in range(strips):
            source = jnp.broadcast_to(rows[tile][c][sub : sub + 1], (8, 128))
            for i in range(tile, tiles):
                weight = jnp.where(row > sub, factor[i], 0.0) if i == tile else factor[i]
                rows[i][c] = rows[i][c] - weight * source
    out = []
    for i in range(tiles):
        scale = lax.rsqrt(pivots[i])
        out.append(jnp.concatenate([rows[i][c] * scale for c in range(strips)], axis=1))
    return jnp.concatenate(out, axis=0)


def factor_block(A):
    same = iota((BLOCK, BLOCK), 0) == iota((BLOCK, BLOCK), 1)
    V = jnp.concatenate([A, onehot(same, F32)], axis=1)
    done = []
    for at in range(0, BLOCK, GROUP):
        rows = pivot_rows(V[:GROUP, at : at + GROUP], V[:GROUP])
        done.append(rows)
        if at + GROUP < BLOCK:
            hi, lo = split(rows)
            here = jnp.concatenate([hi, hi, lo], axis=0)[:, at + GROUP : BLOCK]
            V = V[GROUP:] - dot_t(here, jnp.concatenate([hi, lo, hi], axis=0))
    both = jnp.concatenate(done, axis=0)
    return both[:, :BLOCK], both[:, BLOCK:]


def factor_kernel(all_ref, fac_ref, mine_ref, quad_ref, high, low):
    docs, n = all_ref.shape
    width = n + 128
    replica = lax.axis_index("rep")
    mine = all_ref[pl.ds(pl.multiple_of(replica * BAL, BAL), BAL), :]
    mine_ref[...] = mine
    ri, ci = iota((BLOCK, BLOCK), 0), iota((BLOCK, BLOCK), 1)
    quad = jnp.zeros((1, 128), F32)
    for a in range(0, n, BLOCK):
        b = a + BLOCK
        hessian = dot_t(all_ref[:, a:b], all_ref[:, a:n]) * (1.0 / docs)
        extra = mine[:, a:b].astype(F32).T
        extra = jnp.concatenate([extra, jnp.zeros((BLOCK, 128 - BAL), F32)], axis=1)
        panel = jnp.concatenate([hessian, extra], axis=1)
        if a > 0:
            lh, ll = high[:a, a:b], low[:a, a:b]
            gh, gl = high[:a, a:width], low[:a, a:width]
            panel = panel - (dot_t(lh, gh) + dot_t(lh, gl) + dot_t(ll, gh))
        upper, inverse = factor_block(panel[:, :BLOCK] + jnp.where(ri == ci, DAMPING, 0.0))
        fac_ref[a:b, a:b] = jnp.where(ci >= ri, upper, 0.0)
        th, tl = split(inverse)
        sh, sl = split(panel[:, BLOCK:])
        solved = dot(th, sh) + dot(th, sl) + dot(tl, sh)
        if b < n:
            fac_ref[a:b, b:n] = solved[:, : n - b]
            hi, lo = split(solved)
            high[a:b, b:width] = hi
            low[a:b, b:width] = lo
        if a > 0:
            fac_ref[a:b, :a] = jnp.zeros((BLOCK, a), F32)
        tail = solved[:, n - b :]
        quad = quad + jnp.sum(tail * tail, axis=0, keepdims=True)
    quad_ref[...] = jnp.broadcast_to(quad * (1.0 / n), quad_ref.shape)


def factor(everyone):
    docs, n = everyone.shape
    return pl.pallas_call(
        factor_kernel,
        out_shape=(
            jax.ShapeDtypeStruct((n, n), F32),
            jax.ShapeDtypeStruct((BAL, n), BF16),
            jax.ShapeDtypeStruct((8, 128), F32),
        ),
        in_specs=[VMEM],
        out_specs=(VMEM, VMEM, VMEM),
        scratch_shapes=[pltpu.VMEM((n, n + 128), BF16), pltpu.VMEM((n, n + 128), BF16)],
        compiler_params=pltpu.CompilerParams(vmem_limit_bytes=40 * 2**20),
    )(everyone)


def layer_sum_kernel(layers, quad_ref, out_ref, inbox, send, recv):
    me = lax.axis_index("layer")
    barrier = pltpu.get_barrier_semaphore()
    for step in range(1, layers):
        device = (me + step) % layers
        pl.semaphore_signal(barrier, inc=1, device_id={"layer": device}, device_id_type=pl.DeviceIdType.MESH)
    pl.semaphore_wait(barrier, layers - 1)
    copies = []
    for step in range(1, layers):
        copies.append(
            pltpu.make_async_remote_copy(
                src_ref=quad_ref, dst_ref=inbox.at[step - 1], send_sem=send.at[step - 1],
                recv_sem=recv.at[step - 1], device_id={"layer": (me + step) % layers},
                device_id_type=pl.DeviceIdType.MESH,
            )
        )
        copies[-1].start()
    total = quad_ref[...]
    for step, c in enumerate(copies):
        c.wait_recv()
        total = total + inbox[step]
    out_ref[...] = total[:1, :BAL]
    for c in copies:
        c.wait_send()


def layer_sum(quad, layers):
    return pl.pallas_call(
        functools.partial(layer_sum_kernel, layers),
        out_shape=jax.ShapeDtypeStruct((1, BAL), F32),
        in_specs=[VMEM],
        out_specs=VMEM,
        scratch_shapes=[
            pltpu.VMEM((layers - 1,) + quad.shape, F32),
            pltpu.SemaphoreType.DMA((layers - 1,)),
            pltpu.SemaphoreType.DMA((layers - 1,)),
        ],
        compiler_params=pltpu.CompilerParams(
            collective_id=1, has_side_effects=True, vmem_limit_bytes=2 * 2**20
        ),
    )(quad)


def on_device(n_rep, layers, activations, output_grads, in_projection, out_projection, segment_ids, move_list):
    arranged, aux = front(
        activations[0], output_grads[0], in_projection[0], out_projection[0],
        segment_ids[None], move_list[None],
    )
    everyone = gather(arranged, aux, n_rep)
    upper, mine, quad = factor(everyone)
    influence = layer_sum(quad, layers)
    return (upper[None], mine[None], influence[0])


def solution(mesh):
    placed = (
        PartitionSpec("layer", "rep", None),
        PartitionSpec("layer", "rep", None),
        PartitionSpec("layer", None, None),
        PartitionSpec("layer", None, None),
        PartitionSpec("rep"),
        PartitionSpec("rep"),
    )
    return jax.shard_map(
        functools.partial(on_device, mesh.shape["rep"], mesh.shape["layer"]),
        mesh=mesh,
        in_specs=placed,
        out_specs=(PartitionSpec("layer", None, None), PartitionSpec("layer", "rep", None), PartitionSpec("rep")),
        check_vma=False,
    )
```

```python
import functools

import jax
import jax.numpy as jnp
from jax import lax
from jax.experimental import pallas as pl
from jax.experimental.pallas import tpu as pltpu
from jax.sharding import PartitionSpec

BAL = 32
BLOCK = 128
GROUP = 32
DAMPING = 0.05
F32 = jnp.float32
BF16 = jnp.bfloat16
VMEM = pl.BlockSpec(memory_space=pltpu.VMEM)


def split(x):
    hi = x.astype(BF16)
    lo = (x - hi.astype(F32)).astype(BF16)
    return hi, lo


def dot_t(a, b):
    return lax.dot_general(a, b, (((0,), (0,)), ((), ())), preferred_element_type=F32)


def dot(a, b):
    return lax.dot_general(a, b, (((1,), (0,)), ((), ())), preferred_element_type=F32)


def iota(shape, axis):
    return lax.broadcasted_iota(jnp.int32, shape, axis)


def onehot(mask, dtype=BF16):
    return jnp.where(mask, 1.0, 0.0).astype(dtype)

CHUNKS = (64, 128, 128, 128, 64)
AHEAD = 2


def project(block, proj):
    contract = (((1,), (1,)), ((), ()))
    return lax.dot_general(block, proj, contract, preferred_element_type=F32).astype(BF16)


def expand(x, pattern):
    return dot(x, pattern)


def front_kernel(
    acts_hbm, grads_hbm, in_hbm, out_hbm, segs_hbm, moves_hbm, arr_ref, aux_ref,
    acts, grads, in_proj, out_proj, segs, moves_in, sums, counts, moves_pad, sem, small_sem,
):
    replica = lax.axis_index("rep")
    kin, kout = in_proj.shape[0], out_proj.shape[0]
    slots, width = sums.shape
    doc_slots = moves_in.shape[1]
    small = [
        pltpu.make_async_copy(a, b, small_sem.at[i])
        for i, (a, b) in enumerate(
            ((in_hbm, in_proj), (out_hbm, out_proj), (segs_hbm, segs), (moves_hbm, moves_in))
        )
    ]
    large = []
    ends = [sum(CHUNKS[: c + 1]) for c in range(len(CHUNKS))]
    for c, size in enumerate(CHUNKS):
        rows = pl.ds(ends[c] - size, size)
        large.append(
            (
                pltpu.make_async_copy(acts_hbm.at[rows], acts.at[rows], sem.at[0, c]),
                pltpu.make_async_copy(grads_hbm.at[rows], grads.at[rows], sem.at[1, c]),
            )
        )
    small[0].start()
    small[1].start()
    for pair in large[:AHEAD]:
        pair[0].start()
        pair[1].start()
    small[2].start()
    small[3].start()
    lane, sub = iota((kin, width), 1), iota((kin, width), 0)
    spread = onehot(lane // kout == sub)
    lane, sub = iota((kout, width), 1), iota((kout, width), 0)
    repeat = onehot(lane % kout == sub)
    moves_pad[...] = jnp.full_like(moves_pad, -1)
    def gather_documents(c, left, right):
        hi, lo = split(expand(left, spread) * expand(right, repeat))
        size = CHUNKS[c]
        here = segs[:, ends[c] - size : ends[c]]
        slot = iota((slots, size), 0)
        slot = jnp.where(slot == doc_slots, -1, slot)
        member = onehot(slot == here, F32)
        member_low = member.astype(BF16)
        part = dot(member_low, hi) + dot(member_low, lo)
        number = jnp.broadcast_to(jnp.sum(member, axis=1, keepdims=True), counts.shape)
        if c == 0:
            sums[...] = part
            counts[...] = number
        else:
            sums[...] += part
            counts[...] += number

    held = None
    for copy in small:
        copy.wait()
    for c, size in enumerate(CHUNKS):
        rows = pl.ds(ends[c] - size, size)
        for copy in large[c]:
            copy.wait()
        if c + AHEAD < len(CHUNKS):
            for copy in large[c + AHEAD]:
                copy.start()
        left = project(acts[rows, :], in_proj[...])
        right = project(grads[rows, :], out_proj[...])
        if c > 0:
            gather_documents(c - 1, *held)
        held = left, right
    gather_documents(len(CHUNKS) - 1, *held)
    moves_pad[:, :doc_slots] = moves_in[...]
    total, count = sums[...], counts[...]
    moves = moves_pad[...]
    last = jnp.max(segs[...], axis=1, keepdims=True)
    lanes = moves.shape[1]
    scale = 1.0 / jnp.sqrt(jnp.maximum(count, 1.0))
    scale = jnp.concatenate([scale] * (width // scale.shape[1]), axis=1)
    local = (total * scale).astype(BF16)
    local = jnp.concatenate([local, jnp.zeros((lanes - slots, width), BF16)], axis=0)
    row, slot = iota((3 * BAL, lanes), 0), iota((3 * BAL, lanes), 1)
    offset = jnp.where(row < BAL, 0, jnp.where(row < 2 * BAL, -1, 1))
    target = (replica + offset) * BAL + row % BAL
    chosen = (moves == target) & (moves >= 0) & (slot != last)
    arr_ref[...] = dot(onehot(chosen), local).astype(BF16)
    is_last = iota((slots, width), 0) == last
    last_sum = jnp.sum(jnp.where(is_last, total, 0.0), axis=0, keepdims=True)
    is_last = iota(counts.shape, 0) == last
    last_count = jnp.sum(jnp.where(is_last, count, 0.0), axis=0, keepdims=True)
    goes_to = jnp.sum(jnp.where(iota(moves.shape, 1) == last, moves, 0), axis=1, keepdims=True)
    row = iota((8, width), 0)
    wide = [last_sum, total[doc_slots : doc_slots + 1]]
    wide += [jnp.broadcast_to(v[:, :1], (1, width)) for v in (last_count, count[doc_slots : doc_slots + 1])]
    wide += [jnp.broadcast_to(goes_to.astype(F32), (1, width))]
    aux = jnp.zeros((8, width), F32)
    for i, v in enumerate(wide):
        aux = jnp.where(row == i, v, aux)
    aux_ref[...] = aux


def gather_kernel(side, cores, *refs):
    held, all_ref, work, refs = refs[:6], refs[6], refs[7:18], refs[18:]
    arr_ref, aux_ref, from_right, from_left, aux_in, ex_send, ex_recv, send, recv = refs
    n_rep = side * side * cores
    width = all_ref.shape[1]
    me = lax.axis_index("rep")
    core = me % cores
    spot_z = (me // cores) % side
    spot_x = me // (cores * side)

    def rep_at(dx, dz, c):
        x, z = (spot_x + dx + side) % side, (spot_z + dz + side) % side
        return (x * side + z) * cores + c

    right, left, left2 = (me + 1) % n_rep, (me + n_rep - 1) % n_rep, (me + n_rep - 2) % n_rep
    right2 = (me + 2) % n_rep
    sibling = rep_at(0, 0, 1 - core)
    around = [rep_at(d, 0, core) for d in (1, -1, 2)] + [rep_at(0, d, core) for d in (1, -1, 2)]
    barrier = pltpu.get_barrier_semaphore()
    senders = [right, left, right2, sibling] + around
    for device in senders:
        pl.semaphore_signal(barrier, inc=1, device_id={"rep": device}, device_id_type=pl.DeviceIdType.MESH)
    front_kernel(*held, arr_ref, aux_ref, *work)
    pl.semaphore_wait(barrier, len(senders))

    def copy(src, dst, s, r, device):
        return pltpu.make_async_remote_copy(
            src_ref=src, dst_ref=dst, send_sem=s, recv_sem=r,
            device_id={"rep": device}, device_id_type=pl.DeviceIdType.MESH,
        )

    first = [
        copy(aux_ref, aux_in.at[0], ex_send.at[0], ex_recv.at[0], left),
        copy(aux_ref, aux_in.at[1], ex_send.at[1], ex_recv.at[1], right),
        copy(aux_ref, aux_in.at[2], ex_send.at[2], ex_recv.at[2], left2),
        copy(arr_ref.at[pl.ds(BAL, BAL)], from_right, ex_send.at[3], ex_recv.at[3], left),
        copy(arr_ref.at[pl.ds(2 * BAL, BAL)], from_left, ex_send.at[4], ex_recv.at[4], right),
    ]
    for c in first:
        c.start()
    for c in first:
        c.wait_recv()

    mine = arr_ref[pl.ds(0, BAL), :].astype(F32) + from_right[...].astype(F32) + from_left[...].astype(F32)
    own = aux_ref[...]
    after, before, after2 = aux_in[0], aux_in[1], aux_in[2]
    row = iota((BAL, width), 0).astype(F32)
    base = (me * BAL).astype(F32)
    for a, b in ((before, own), (own, after), (after, after2)):
        length = jnp.maximum(a[2:3] + b[3:4], 1.0)
        feature = (a[0:1] + b[1:2]) * (1.0 / jnp.sqrt(length))
        mine = jnp.where(row == a[4:5] - base, feature, mine)
    all_ref[pl.ds(pl.multiple_of(me * BAL, BAL), BAL), :] = mine.astype(BF16)

    half = width // 2
    sent = []

    def piece(dx, dz, c, col, cols):
        start = pl.multiple_of(rep_at(dx, dz, c) * BAL, BAL)
        return all_ref.at[pl.ds(start, BAL), pl.ds(col, cols)]

    def start(index, dx, dz, col, cols, device):
        ref = piece(dx, dz, core, col, cols)
        c = copy(ref, ref, send.at[index], recv.at[index], device)
        c.start()
        sent.append(c)

    def arrived(index, dx, dz, c, col, cols):
        ref = piece(dx, dz, c, col, cols)
        copy(ref, ref, send.at[index], recv.at[index], sibling).wait_recv()

    def place(kind, du, dv):
        return (du, dv) if kind == 0 else (dv, du)

    def to(kind, du, dv):
        return rep_at(*place(kind, du, dv), core)

    order = (0, 1, -1, 2)
    per_kind = 3 + 12 + 16

    def along(kind):
        for i, d in enumerate(order[1:]):
            start(kind * per_kind + i, 0, 0, kind * half, half, to(kind, d, 0))

    def across(kind, du):
        at = place(kind, du, 0)
        for i, d in enumerate(order[1:]):
            n = kind * per_kind + 3 + 3 * order.index(du) + i
            start(n, *at, kind * half, half, to(kind, 0, d))

    def share(kind, du, dv):
        n = kind * per_kind + 15 + 4 * order.index(du) + order.index(dv)
        start(n, *place(kind, du, dv), kind * half, half, sibling)

    def back(d):
        return d if d == 2 else -d

    for kind in (0, 1):
        along(kind)
    for kind in (0, 1):
        across(kind, 0)
        share(kind, 0, 0)
    for i, d in enumerate(order[1:]):
        for kind in (0, 1):
            arrived(kind * per_kind + i, *place(kind, back(d), 0), core, kind * half, half)
            across(kind, back(d))
            share(kind, back(d), 0)
    for du in (0, -1, 1, 2):
        for i, d in enumerate(order[1:]):
            for kind in (0, 1):
                n = kind * per_kind + 3 + 3 * order.index(du) + i
                arrived(n, *place(kind, du, back(d)), core, kind * half, half)
                share(kind, du, back(d))
    for kind in (0, 1):
        for i, du in enumerate(order):
            for j, dv in enumerate(order):
                n = kind * per_kind + 15 + 4 * i + j
                arrived(n, *place(kind, du, dv), 1 - core, kind * half, half)
    for c in first + sent:
        c.wait_send()


def gather(acts, grads, in_proj, out_proj, segs, moves, n_rep):
    kin, kout = in_proj.shape[0], out_proj.shape[0]
    width = kin * kout
    slots = -(-(moves.shape[1] + 1) // 16) * 16
    cores = 2
    side = round((n_rep // cores) ** 0.5)
    held = [
        pltpu.with_memory_space_constraint(v, pltpu.HBM)
        for v in (acts, grads, in_proj, out_proj, segs, moves)
    ]
    return pl.pallas_call(
        functools.partial(gather_kernel, side, cores),
        out_shape=jax.ShapeDtypeStruct((BAL * n_rep, width), BF16),
        in_specs=[pl.BlockSpec(memory_space=pltpu.HBM)] * 6,
        out_specs=VMEM,
        scratch_shapes=[
            pltpu.VMEM(acts.shape, BF16),
            pltpu.VMEM(grads.shape, BF16),
            pltpu.VMEM(in_proj.shape, BF16),
            pltpu.VMEM(out_proj.shape, BF16),
            pltpu.VMEM(segs.shape, jnp.int32),
            pltpu.VMEM(moves.shape, jnp.int32),
            pltpu.VMEM((slots, width), F32),
            pltpu.VMEM((slots, 128), F32),
            pltpu.VMEM((1, 128), jnp.int32),
            pltpu.SemaphoreType.DMA((2, len(CHUNKS))),
            pltpu.SemaphoreType.DMA((4,)),
            pltpu.VMEM((3 * BAL, width), BF16),
            pltpu.VMEM((8, width), F32),
            pltpu.VMEM((BAL, width), BF16),
            pltpu.VMEM((BAL, width), BF16),
            pltpu.VMEM((3, 8, width), F32),
            pltpu.SemaphoreType.DMA((5,)),
            pltpu.SemaphoreType.DMA((5,)),
            pltpu.SemaphoreType.DMA((62,)),
            pltpu.SemaphoreType.DMA((62,)),
        ],
        compiler_params=pltpu.CompilerParams(
            collective_id=0, has_side_effects=True, vmem_limit_bytes=40 * 2**20
        ),
    )(*held)

SUB = 16

def pivot_rows(V, at):
    size, width = V.shape
    tiles, strips = size // 8, width // 128
    row = iota((8, 128), 0)
    rows = [[V[8 * i : 8 * i + 8, 128 * c : 128 * c + 128] for c in range(strips)] for i in range(tiles)]
    pivots = [jnp.ones((8, 128), F32) for _ in range(tiles)]
    cols = {}

    def element(column, j):
        return jnp.broadcast_to(column[j // 8][j % 8 : j % 8 + 1], (8, 128))

    for j in range(0, size, 2):
        tile, sub = divmod(j, 8)
        if j % SUB == 0:
            for k in range(j, j + SUB):
                lanes = slice(at + k, at + k + 1)
                cols[k] = [
                    jnp.broadcast_to(rows[i][0][:, lanes], (8, 128)) if i >= k // 8 else None for i in range(tiles)
                ]
        one, two = cols[j], cols[j + 1]
        p, q, r = element(one, j), element(one, j + 1), element(two, j + 1)
        det = p * r - q * q
        inv_p = 1.0 / p
        inv_det = 1.0 / det
        ratio = q * inv_p
        second = p * inv_det
        pivots[tile] = jnp.where(row == sub, p, pivots[tile])
        pivots[tile] = jnp.where(row == sub + 1, det * inv_p, pivots[tile])
        left = [None] * tiles
        right = [None] * tiles
        rest = [None] * tiles
        for i in range(tile, tiles):
            rest[i] = two[i] - one[i] * ratio
            left[i] = one[i] * inv_p
            right[i] = rest[i] * second
        for j2 in range(j + 2, j - j % SUB + SUB):
            mul_one, mul_two = element(one, j2), element(rest, j2)
            for i in range(j2 // 8, tiles):
                cols[j2][i] = (cols[j2][i] - left[i] * mul_one) - right[i] * mul_two
        for c in range(strips):
            top = jnp.broadcast_to(rows[tile][c][sub : sub + 1], (8, 128))
            next_row = jnp.broadcast_to(rows[tile][c][sub + 1 : sub + 2], (8, 128)) - top * ratio
            for i in range(tile, tiles):
                if i == tile:
                    wl = jnp.where(row > sub, left[i], 0.0)
                    wr = jnp.where(row > sub + 1, right[i], 0.0)
                else:
                    wl, wr = left[i], right[i]
                rows[i][c] = (rows[i][c] - wl * top) - wr * next_row
    out = []
    for i in range(tiles):
        scale = lax.rsqrt(pivots[i])
        out.append(jnp.concatenate([rows[i][c] * scale for c in range(strips)], axis=1))
    return jnp.concatenate(out, axis=0)


def factor_block(A):
    same = iota((BLOCK, BLOCK), 0) == iota((BLOCK, BLOCK), 1)
    V = jnp.concatenate([A, onehot(same, F32)], axis=1)
    done = []
    for at in range(0, BLOCK, GROUP):
        rows = pivot_rows(V[:GROUP], at)
        done.append(rows)
        if at + GROUP < BLOCK:
            hi, lo = split(rows)
            here = jnp.concatenate([hi, hi, lo], axis=0)[:, at + GROUP : BLOCK]
            V = V[GROUP:] - dot_t(here, jnp.concatenate([hi, lo, hi], axis=0))
    both = jnp.concatenate(done, axis=0)
    return both[:, :BLOCK], both[:, BLOCK:]


def factor_kernel(all_ref, fac_ref, mine_ref, quad_ref, high, low):
    docs, n = all_ref.shape
    width = n + 128
    replica = lax.axis_index("rep")
    mine = all_ref[pl.ds(pl.multiple_of(replica * BAL, BAL), BAL), :]
    mine_ref[...] = mine
    ri, ci = iota((BLOCK, BLOCK), 0), iota((BLOCK, BLOCK), 1)
    quad = jnp.zeros((1, 128), F32)
    for a in range(0, n, BLOCK):
        b = a + BLOCK
        hessian = dot_t(all_ref[:, a:b], all_ref[:, a:n]) * (1.0 / docs)
        extra = mine[:, a:b].astype(F32).T
        extra = jnp.concatenate([extra, jnp.zeros((BLOCK, 128 - BAL), F32)], axis=1)
        panel = jnp.concatenate([hessian, extra], axis=1)
        if a > 0:
            lh, ll = high[:a, a:b], low[:a, a:b]
            gh, gl = high[:a, a:width], low[:a, a:width]
            panel = panel - (dot_t(lh, gh) + dot_t(lh, gl) + dot_t(ll, gh))
        upper, inverse = factor_block(panel[:, :BLOCK] + jnp.where(ri == ci, DAMPING, 0.0))
        fac_ref[a:b, a:b] = jnp.where(ci >= ri, upper, 0.0)
        th, tl = split(inverse)
        sh, sl = split(panel[:, BLOCK:])
        solved = dot(th, sh) + dot(th, sl) + dot(tl, sh)
        if b < n:
            fac_ref[a:b, b:n] = solved[:, : n - b]
            hi, lo = split(solved)
            high[a:b, b:width] = hi
            low[a:b, b:width] = lo
        if a > 0:
            fac_ref[a:b, :a] = jnp.zeros((BLOCK, a), F32)
        tail = solved[:, n - b :]
        quad = quad + jnp.sum(tail * tail, axis=0, keepdims=True)
    quad_ref[...] = jnp.broadcast_to(quad * (1.0 / n), quad_ref.shape)


def factor(everyone):
    docs, n = everyone.shape
    return pl.pallas_call(
        factor_kernel,
        out_shape=(
            jax.ShapeDtypeStruct((n, n), F32),
            jax.ShapeDtypeStruct((BAL, n), BF16),
            jax.ShapeDtypeStruct((8, 128), F32),
        ),
        in_specs=[VMEM],
        out_specs=(VMEM, VMEM, VMEM),
        scratch_shapes=[pltpu.VMEM((n, n + 128), BF16), pltpu.VMEM((n, n + 128), BF16)],
        compiler_params=pltpu.CompilerParams(vmem_limit_bytes=40 * 2**20),
    )(everyone)


def layer_sum_kernel(layers, quad_ref, out_ref, inbox, send, recv):
    me = lax.axis_index("layer")
    barrier = pltpu.get_barrier_semaphore()
    for step in range(1, layers):
        device = (me + step) % layers
        pl.semaphore_signal(barrier, inc=1, device_id={"layer": device}, device_id_type=pl.DeviceIdType.MESH)
    pl.semaphore_wait(barrier, layers - 1)
    copies = []
    for step in range(1, layers):
        copies.append(
            pltpu.make_async_remote_copy(
                src_ref=quad_ref, dst_ref=inbox.at[step - 1], send_sem=send.at[step - 1],
                recv_sem=recv.at[step - 1], device_id={"layer": (me + step) % layers},
                device_id_type=pl.DeviceIdType.MESH,
            )
        )
        copies[-1].start()
    total = quad_ref[...]
    for step, c in enumerate(copies):
        c.wait_recv()
        total = total + inbox[step]
    out_ref[...] = total[:1, :BAL]
    for c in copies:
        c.wait_send()


def layer_sum(quad, layers):
    return pl.pallas_call(
        functools.partial(layer_sum_kernel, layers),
        out_shape=jax.ShapeDtypeStruct((1, BAL), F32),
        in_specs=[VMEM],
        out_specs=VMEM,
        scratch_shapes=[
            pltpu.VMEM((layers - 1,) + quad.shape, F32),
            pltpu.SemaphoreType.DMA((layers - 1,)),
            pltpu.SemaphoreType.DMA((layers - 1,)),
        ],
        compiler_params=pltpu.CompilerParams(
            collective_id=1, has_side_effects=True, vmem_limit_bytes=2 * 2**20
        ),
    )(quad)


def on_device(n_rep, layers, activations, output_grads, in_projection, out_projection, segment_ids, move_list):
    everyone = gather(
        activations[0], output_grads[0], in_projection[0], out_projection[0],
        segment_ids[None], move_list[None], n_rep,
    )
    upper, mine, quad = factor(everyone)
    influence = layer_sum(quad, layers)
    return (upper[None], mine[None], influence[0])


def solution(mesh):
    placed = (
        PartitionSpec("layer", "rep", None),
        PartitionSpec("layer", "rep", None),
        PartitionSpec("layer", None, None),
        PartitionSpec("layer", None, None),
        PartitionSpec("rep"),
        PartitionSpec("rep"),
    )
    return jax.shard_map(
        functools.partial(on_device, mesh.shape["rep"], mesh.shape["layer"]),
        mesh=mesh,
        in_specs=placed,
        out_specs=(PartitionSpec("layer", None, None), PartitionSpec("layer", "rep", None), PartitionSpec("rep")),
        check_vma=False,
    )
```

```python
import functools

import jax
import jax.numpy as jnp
from jax import lax
from jax.experimental import pallas as pl
from jax.experimental.pallas import tpu as pltpu
from jax.sharding import PartitionSpec

BAL = 32
BLOCK = 128
GROUP = 32
DAMPING = 0.05
F32 = jnp.float32
BF16 = jnp.bfloat16
VMEM = pl.BlockSpec(memory_space=pltpu.VMEM)


def split(x):
    hi = x.astype(BF16)
    lo = (x - hi.astype(F32)).astype(BF16)
    return hi, lo


def dot_t(a, b):
    return lax.dot_general(a, b, (((0,), (0,)), ((), ())), preferred_element_type=F32)


def dot(a, b):
    return lax.dot_general(a, b, (((1,), (0,)), ((), ())), preferred_element_type=F32)


def iota(shape, axis):
    return lax.broadcasted_iota(jnp.int32, shape, axis)


def onehot(mask, dtype=BF16):
    return jnp.where(mask, 1.0, 0.0).astype(dtype)

CHUNKS = (64, 128, 128, 128, 64)
AHEAD = 2


def project(block, proj):
    contract = (((1,), (1,)), ((), ()))
    return lax.dot_general(block, proj, contract, preferred_element_type=F32).astype(BF16)


def expand(x, pattern):
    return dot(x, pattern)


def front_kernel(
    acts_hbm, grads_hbm, in_hbm, out_hbm, segs_hbm, moves_hbm, arr_ref, aux_ref,
    acts, grads, in_proj, out_proj, segs, moves_in, sums, counts, moves_pad, sem, small_sem,
):
    replica = lax.axis_index("rep")
    kin, kout = in_proj.shape[0], out_proj.shape[0]
    slots, width = sums.shape
    doc_slots = moves_in.shape[1]
    small = [
        pltpu.make_async_copy(a, b, small_sem.at[i])
        for i, (a, b) in enumerate(
            ((in_hbm, in_proj), (out_hbm, out_proj), (segs_hbm, segs), (moves_hbm, moves_in))
        )
    ]
    large = []
    ends = [sum(CHUNKS[: c + 1]) for c in range(len(CHUNKS))]
    for c, size in enumerate(CHUNKS):
        rows = pl.ds(ends[c] - size, size)
        large.append(
            (
                pltpu.make_async_copy(acts_hbm.at[rows], acts.at[rows], sem.at[0, c]),
                pltpu.make_async_copy(grads_hbm.at[rows], grads.at[rows], sem.at[1, c]),
            )
        )
    small[0].start()
    small[1].start()
    for pair in large[:AHEAD]:
        pair[0].start()
        pair[1].start()
    small[2].start()
    small[3].start()
    lane, sub = iota((kin, width), 1), iota((kin, width), 0)
    spread = onehot(lane // kout == sub)
    lane, sub = iota((kout, width), 1), iota((kout, width), 0)
    repeat = onehot(lane % kout == sub)
    moves_pad[...] = jnp.full_like(moves_pad, -1)
    def gather_documents(c, left, right):
        hi, lo = split(expand(left, spread) * expand(right, repeat))
        size = CHUNKS[c]
        here = segs[:, ends[c] - size : ends[c]]
        slot = iota((slots, size), 0)
        slot = jnp.where(slot == doc_slots, -1, slot)
        member = onehot(slot == here, F32)
        member_low = member.astype(BF16)
        part = dot(member_low, hi) + dot(member_low, lo)
        number = jnp.broadcast_to(jnp.sum(member, axis=1, keepdims=True), counts.shape)
        if c == 0:
            sums[...] = part
            counts[...] = number
        else:
            sums[...] += part
            counts[...] += number

    held = None
    for copy in small:
        copy.wait()
    for c, size in enumerate(CHUNKS):
        rows = pl.ds(ends[c] - size, size)
        for copy in large[c]:
            copy.wait()
        if c + AHEAD < len(CHUNKS):
            for copy in large[c + AHEAD]:
                copy.start()
        left = project(acts[rows, :], in_proj[...])
        right = project(grads[rows, :], out_proj[...])
        if c > 0:
            gather_documents(c - 1, *held)
        held = left, right
    gather_documents(len(CHUNKS) - 1, *held)
    moves_pad[:, :doc_slots] = moves_in[...]
    total, count = sums[...], counts[...]
    moves = moves_pad[...]
    last = jnp.max(segs[...], axis=1, keepdims=True)
    lanes = moves.shape[1]
    scale = 1.0 / jnp.sqrt(jnp.maximum(count, 1.0))
    scale = jnp.concatenate([scale] * (width // scale.shape[1]), axis=1)
    local = (total * scale).astype(BF16)
    local = jnp.concatenate([local, jnp.zeros((lanes - slots, width), BF16)], axis=0)
    row, slot = iota((3 * BAL, lanes), 0), iota((3 * BAL, lanes), 1)
    offset = jnp.where(row < BAL, 0, jnp.where(row < 2 * BAL, -1, 1))
    target = (replica + offset) * BAL + row % BAL
    chosen = (moves == target) & (moves >= 0) & (slot != last)
    arr_ref[...] = dot(onehot(chosen), local).astype(BF16)
    is_last = iota((slots, width), 0) == last
    last_sum = jnp.sum(jnp.where(is_last, total, 0.0), axis=0, keepdims=True)
    is_last = iota(counts.shape, 0) == last
    last_count = jnp.sum(jnp.where(is_last, count, 0.0), axis=0, keepdims=True)
    goes_to = jnp.sum(jnp.where(iota(moves.shape, 1) == last, moves, 0), axis=1, keepdims=True)
    row = iota((8, width), 0)
    wide = [last_sum, total[doc_slots : doc_slots + 1]]
    wide += [jnp.broadcast_to(v[:, :1], (1, width)) for v in (last_count, count[doc_slots : doc_slots + 1])]
    wide += [jnp.broadcast_to(goes_to.astype(F32), (1, width))]
    aux = jnp.zeros((8, width), F32)
    for i, v in enumerate(wide):
        aux = jnp.where(row == i, v, aux)
    aux_ref[...] = aux


def gather_kernel(side, cores, *refs):
    held, all_ref, work, refs = refs[:6], refs[6], refs[7:18], refs[18:]
    arr_ref, aux_ref, from_right, from_left, aux_in, ex_send, ex_recv, send, recv = refs
    n_rep = side * side * cores
    width = all_ref.shape[1]
    me = lax.axis_index("rep")
    core = me % cores
    spot_z = (me // cores) % side
    spot_x = me // (cores * side)

    def rep_at(dx, dz, c):
        x, z = (spot_x + dx + side) % side, (spot_z + dz + side) % side
        return (x * side + z) * cores + c

    right, left, left2 = (me + 1) % n_rep, (me + n_rep - 1) % n_rep, (me + n_rep - 2) % n_rep
    right2 = (me + 2) % n_rep
    sibling = rep_at(0, 0, 1 - core)
    around = [rep_at(d, 0, core) for d in (1, -1, 2)] + [rep_at(0, d, core) for d in (1, -1, 2)]
    barrier = pltpu.get_barrier_semaphore()
    senders = [right, left, right2, sibling] + around
    for device in senders:
        pl.semaphore_signal(barrier, inc=1, device_id={"rep": device}, device_id_type=pl.DeviceIdType.MESH)
    front_kernel(*held, arr_ref, aux_ref, *work)
    pl.semaphore_wait(barrier, len(senders))

    def copy(src, dst, s, r, device):
        return pltpu.make_async_remote_copy(
            src_ref=src, dst_ref=dst, send_sem=s, recv_sem=r,
            device_id={"rep": device}, device_id_type=pl.DeviceIdType.MESH,
        )

    first = [
        copy(aux_ref, aux_in.at[0], ex_send.at[0], ex_recv.at[0], left),
        copy(aux_ref, aux_in.at[1], ex_send.at[1], ex_recv.at[1], right),
        copy(aux_ref, aux_in.at[2], ex_send.at[2], ex_recv.at[2], left2),
        copy(arr_ref.at[pl.ds(BAL, BAL)], from_right, ex_send.at[3], ex_recv.at[3], left),
        copy(arr_ref.at[pl.ds(2 * BAL, BAL)], from_left, ex_send.at[4], ex_recv.at[4], right),
    ]
    for c in first:
        c.start()
    for c in first:
        c.wait_recv()

    mine = arr_ref[pl.ds(0, BAL), :].astype(F32) + from_right[...].astype(F32) + from_left[...].astype(F32)
    own = aux_ref[...]
    after, before, after2 = aux_in[0], aux_in[1], aux_in[2]
    row = iota((BAL, width), 0).astype(F32)
    base = (me * BAL).astype(F32)
    for a, b in ((before, own), (own, after), (after, after2)):
        length = jnp.maximum(a[2:3] + b[3:4], 1.0)
        feature = (a[0:1] + b[1:2]) * (1.0 / jnp.sqrt(length))
        mine = jnp.where(row == a[4:5] - base, feature, mine)
    all_ref[pl.ds(pl.multiple_of(me * BAL, BAL), BAL), :] = mine.astype(BF16)

    half = width // 2
    sent = []

    def piece(dx, dz, c, col, cols):
        start = pl.multiple_of(rep_at(dx, dz, c) * BAL, BAL)
        return all_ref.at[pl.ds(start, BAL), pl.ds(col, cols)]

    def start(index, dx, dz, col, cols, device):
        ref = piece(dx, dz, core, col, cols)
        c = copy(ref, ref, send.at[index], recv.at[index], device)
        c.start()
        sent.append(c)

    def arrived(index, dx, dz, c, col, cols):
        ref = piece(dx, dz, c, col, cols)
        copy(ref, ref, send.at[index], recv.at[index], sibling).wait_recv()

    def place(kind, du, dv):
        return (du, dv) if kind == 0 else (dv, du)

    def to(kind, du, dv):
        return rep_at(*place(kind, du, dv), core)

    order = (0, 1, -1, 2)
    per_kind = 3 + 12 + 16

    def along(kind):
        for i, d in enumerate(order[1:]):
            start(kind * per_kind + i, 0, 0, kind * half, half, to(kind, d, 0))

    def across(kind, du):
        at = place(kind, du, 0)
        for i, d in enumerate(order[1:]):
            n = kind * per_kind + 3 + 3 * order.index(du) + i
            start(n, *at, kind * half, half, to(kind, 0, d))

    def share(kind, du, dv):
        n = kind * per_kind + 15 + 4 * order.index(du) + order.index(dv)
        start(n, *place(kind, du, dv), kind * half, half, sibling)

    def back(d):
        return d if d == 2 else -d

    for kind in (0, 1):
        along(kind)
    for kind in (0, 1):
        across(kind, 0)
        share(kind, 0, 0)
    for i, d in enumerate(order[1:]):
        for kind in (0, 1):
            arrived(kind * per_kind + i, *place(kind, back(d), 0), core, kind * half, half)
            across(kind, back(d))
            share(kind, back(d), 0)
    for du in (0, -1, 1, 2):
        for i, d in enumerate(order[1:]):
            for kind in (0, 1):
                n = kind * per_kind + 3 + 3 * order.index(du) + i
                arrived(n, *place(kind, du, back(d)), core, kind * half, half)
                share(kind, du, back(d))
    for kind in (0, 1):
        for i, du in enumerate(order):
            for j, dv in enumerate(order):
                n = kind * per_kind + 15 + 4 * i + j
                arrived(n, *place(kind, du, dv), 1 - core, kind * half, half)
    for c in first + sent:
        c.wait_send()


def gather(acts, grads, in_proj, out_proj, segs, moves, n_rep):
    kin, kout = in_proj.shape[0], out_proj.shape[0]
    width = kin * kout
    slots = -(-(moves.shape[1] + 1) // 16) * 16
    cores = 2
    side = round((n_rep // cores) ** 0.5)
    held = [
        pltpu.with_memory_space_constraint(v, pltpu.HBM)
        for v in (acts, grads, in_proj, out_proj, segs, moves)
    ]
    return pl.pallas_call(
        functools.partial(gather_kernel, side, cores),
        out_shape=jax.ShapeDtypeStruct((BAL * n_rep, width), BF16),
        in_specs=[pl.BlockSpec(memory_space=pltpu.HBM)] * 6,
        out_specs=VMEM,
        scratch_shapes=[
            pltpu.VMEM(acts.shape, BF16),
            pltpu.VMEM(grads.shape, BF16),
            pltpu.VMEM(in_proj.shape, BF16),
            pltpu.VMEM(out_proj.shape, BF16),
            pltpu.VMEM(segs.shape, jnp.int32),
            pltpu.VMEM(moves.shape, jnp.int32),
            pltpu.VMEM((slots, width), F32),
            pltpu.VMEM((slots, 128), F32),
            pltpu.VMEM((1, 128), jnp.int32),
            pltpu.SemaphoreType.DMA((2, len(CHUNKS))),
            pltpu.SemaphoreType.DMA((4,)),
            pltpu.VMEM((3 * BAL, width), BF16),
            pltpu.VMEM((8, width), F32),
            pltpu.VMEM((BAL, width), BF16),
            pltpu.VMEM((BAL, width), BF16),
            pltpu.VMEM((3, 8, width), F32),
            pltpu.SemaphoreType.DMA((5,)),
            pltpu.SemaphoreType.DMA((5,)),
            pltpu.SemaphoreType.DMA((62,)),
            pltpu.SemaphoreType.DMA((62,)),
        ],
        compiler_params=pltpu.CompilerParams(
            collective_id=0, has_side_effects=True, vmem_limit_bytes=40 * 2**20
        ),
    )(*held)

AHEAD_COLS = 6
SUB = 8

def pivot_rows(V, at):
    size, width = V.shape
    tiles, strips = size // 8, width // 128
    row = iota((8, 128), 0)
    rows = [[V[8 * i : 8 * i + 8, 128 * c : 128 * c + 128] for c in range(strips)] for i in range(tiles)]
    pivots = [jnp.ones((8, 128), F32) for _ in range(tiles)]
    cols = {}

    def element(column, j):
        return jnp.broadcast_to(column[j // 8][j % 8 : j % 8 + 1], (8, 128))

    def spread(first, stop):
        for k in range(first, stop):
            lanes = slice(at + k, at + k + 1)
            cols[k] = [
                jnp.broadcast_to(rows[i][0][:, lanes], (8, 128)) if i >= k // 8 else None for i in range(tiles)
            ]

    for j in range(0, size, 2):
        tile, sub = divmod(j, 8)
        end = j - j % SUB + SUB
        if j == 0:
            spread(0, SUB)
        if j == end - AHEAD_COLS and end < size:
            spread(end, end + SUB)
        one, two = cols[j], cols[j + 1]
        p, q, r = element(one, j), element(one, j + 1), element(two, j + 1)
        det = p * r - q * q
        inv_p = 1.0 / p
        inv_det = 1.0 / det
        ratio = q * inv_p
        second = p * inv_det
        pivots[tile] = jnp.where(row == sub, p, pivots[tile])
        pivots[tile] = jnp.where(row == sub + 1, det * inv_p, pivots[tile])
        left = [None] * tiles
        right = [None] * tiles
        rest = [None] * tiles
        for i in range(tile, tiles):
            rest[i] = two[i] - one[i] * ratio
            left[i] = one[i] * inv_p
            right[i] = rest[i] * second
        for j2 in [k for k in sorted(cols) if k > j + 1]:
            mul_one, mul_two = element(one, j2), element(rest, j2)
            for i in range(j2 // 8, tiles):
                cols[j2][i] = (cols[j2][i] - left[i] * mul_one) - right[i] * mul_two
        for c in range(strips):
            top = jnp.broadcast_to(rows[tile][c][sub : sub + 1], (8, 128))
            next_row = jnp.broadcast_to(rows[tile][c][sub + 1 : sub + 2], (8, 128)) - top * ratio
            for i in range(tile, tiles):
                if i == tile:
                    wl = jnp.where(row > sub, left[i], 0.0)
                    wr = jnp.where(row > sub + 1, right[i], 0.0)
                else:
                    wl, wr = left[i], right[i]
                rows[i][c] = (rows[i][c] - wl * top) - wr * next_row
    out = []
    for i in range(tiles):
        scale = lax.rsqrt(pivots[i])
        out.append(jnp.concatenate([rows[i][c] * scale for c in range(strips)], axis=1))
    return jnp.concatenate(out, axis=0)


def factor_block(A):
    same = iota((BLOCK, BLOCK), 0) == iota((BLOCK, BLOCK), 1)
    V = jnp.concatenate([A, onehot(same, F32)], axis=1)
    done = []
    for at in range(0, BLOCK, GROUP):
        rows = pivot_rows(V[:GROUP], at)
        done.append(rows)
        if at + GROUP < BLOCK:
            hi, lo = split(rows)
            here = jnp.concatenate([hi, hi, lo], axis=0)
            update = dot_t(here[:, :BLOCK], jnp.concatenate([hi, lo, hi], axis=0))
            V = V[GROUP:] - update[at + GROUP :]
    both = jnp.concatenate(done, axis=0)
    return both[:, :BLOCK], both[:, BLOCK:]


def product(lh, ll, gh, gl):
    left = jnp.concatenate([lh, lh, ll], axis=0)
    return dot_t(left, jnp.concatenate([gh, gl, gh], axis=0))


def solve(inverse, columns):
    th, tl = split(inverse)
    sh, sl = split(columns)
    return dot(jnp.concatenate([th, th, tl], axis=1), jnp.concatenate([sh, sl, sh], axis=0))


def factor_kernel(all_ref, fac_hbm, mine_hbm, quad_ref, fac_ref, high, low, sem):
    docs, n = all_ref.shape
    width = n + 128
    replica = lax.axis_index("rep")
    own = pl.ds(pl.multiple_of(replica * BAL, BAL), BAL)
    mine = all_ref[own, :]
    writes = [pltpu.make_async_copy(all_ref.at[own], mine_hbm, sem.at[n // BLOCK])]
    writes[0].start()
    ri, ci = iota((BLOCK, BLOCK), 0), iota((BLOCK, BLOCK), 1)
    quad = jnp.zeros((1, 128), F32)

    def open_panel(a):
        b, before = a + BLOCK, a - BLOCK
        hessian = dot_t(all_ref[:, a:b], all_ref[:, a:n]) * (1.0 / docs)
        extra = mine[:, a:b].astype(F32).T
        extra = jnp.concatenate([extra, jnp.zeros((BLOCK, 128 - BAL), F32)], axis=1)
        panel = jnp.concatenate([hessian, extra], axis=1)
        if before > 0:
            lh, ll = high[:before, a:b], low[:before, a:b]
            gh, gl = high[:before, a:width], low[:before, a:width]
            panel = panel - (dot_t(lh, gh) + dot_t(lh, gl) + dot_t(ll, gh))
        return panel

    following = open_panel(0)
    for a in range(0, n, BLOCK):
        b = a + BLOCK
        diag, rest = following[:, :BLOCK], following[:, BLOCK:]
        if a > 0:
            lh, ll = hi[:, :BLOCK], lo[:, :BLOCK]
            diag = diag - product(lh, ll, lh, ll)
        if b < n:
            following = open_panel(b)
        upper, inverse = factor_block(diag + jnp.where(ri == ci, DAMPING, 0.0))
        if a > 0:
            rest = rest - product(lh, ll, hi[:, BLOCK:], lo[:, BLOCK:])
        fac_ref[a:b, a:b] = jnp.where(ci >= ri, upper, 0.0)
        parts = [solve(inverse, rest[:, :BLOCK])]
        if b < n:
            parts.append(solve(inverse, rest[:, BLOCK:]))
        solved = jnp.concatenate(parts, axis=1)
        if b < n:
            fac_ref[a:b, b:n] = solved[:, : n - b]
            hi, lo = split(solved)
            high[a:b, b:width] = hi
            low[a:b, b:width] = lo
        if a > 0:
            fac_ref[a:b, :a] = jnp.zeros((BLOCK, a), F32)
        done = pl.ds(a, BLOCK)
        writes.append(pltpu.make_async_copy(fac_ref.at[done], fac_hbm.at[done], sem.at[a // BLOCK]))
        writes[-1].start()
        tail = solved[:, n - b :]
        quad = quad + jnp.sum(tail * tail, axis=0, keepdims=True)
    quad_ref[...] = jnp.broadcast_to(quad * (1.0 / n), quad_ref.shape)
    for write in writes:
        write.wait()


def factor(everyone):
    docs, n = everyone.shape
    return pl.pallas_call(
        factor_kernel,
        out_shape=(
            jax.ShapeDtypeStruct((n, n), F32),
            jax.ShapeDtypeStruct((BAL, n), BF16),
            jax.ShapeDtypeStruct((8, 128), F32),
        ),
        in_specs=[VMEM],
        out_specs=(pl.BlockSpec(memory_space=pltpu.HBM), pl.BlockSpec(memory_space=pltpu.HBM), VMEM),
        scratch_shapes=[
            pltpu.VMEM((n, n), F32),
            pltpu.VMEM((n, n + 128), BF16),
            pltpu.VMEM((n, n + 128), BF16),
            pltpu.SemaphoreType.DMA((n // BLOCK + 1,)),
        ],
        compiler_params=pltpu.CompilerParams(vmem_limit_bytes=40 * 2**20),
    )(everyone)


def layer_sum_kernel(layers, quad_ref, out_ref, inbox, send, recv):
    me = lax.axis_index("layer")
    barrier = pltpu.get_barrier_semaphore()
    for step in range(1, layers):
        device = (me + step) % layers
        pl.semaphore_signal(barrier, inc=1, device_id={"layer": device}, device_id_type=pl.DeviceIdType.MESH)
    pl.semaphore_wait(barrier, layers - 1)
    copies = []
    for step in range(1, layers):
        copies.append(
            pltpu.make_async_remote_copy(
                src_ref=quad_ref, dst_ref=inbox.at[step - 1], send_sem=send.at[step - 1],
                recv_sem=recv.at[step - 1], device_id={"layer": (me + step) % layers},
                device_id_type=pl.DeviceIdType.MESH,
            )
        )
        copies[-1].start()
    total = quad_ref[...]
    for step, c in enumerate(copies):
        c.wait_recv()
        total = total + inbox[step]
    out_ref[...] = total[:1, :BAL]
    for c in copies:
        c.wait_send()


def layer_sum(quad, layers):
    return pl.pallas_call(
        functools.partial(layer_sum_kernel, layers),
        out_shape=jax.ShapeDtypeStruct((1, BAL), F32),
        in_specs=[VMEM],
        out_specs=VMEM,
        scratch_shapes=[
            pltpu.VMEM((layers - 1,) + quad.shape, F32),
            pltpu.SemaphoreType.DMA((layers - 1,)),
            pltpu.SemaphoreType.DMA((layers - 1,)),
        ],
        compiler_params=pltpu.CompilerParams(
            collective_id=1, has_side_effects=True, vmem_limit_bytes=2 * 2**20
        ),
    )(quad)


def on_device(n_rep, layers, activations, output_grads, in_projection, out_projection, segment_ids, move_list):
    everyone = gather(
        activations[0], output_grads[0], in_projection[0], out_projection[0],
        segment_ids[None], move_list[None], n_rep,
    )
    upper, mine, quad = factor(everyone)
    influence = layer_sum(quad, layers)
    return (upper[None], mine[None], influence[0])


def solution(mesh):
    placed = (
        PartitionSpec("layer", "rep", None),
        PartitionSpec("layer", "rep", None),
        PartitionSpec("layer", None, None),
        PartitionSpec("layer", None, None),
        PartitionSpec("rep"),
        PartitionSpec("rep"),
    )
    return jax.shard_map(
        functools.partial(on_device, mesh.shape["rep"], mesh.shape["layer"]),
        mesh=mesh,
        in_specs=placed,
        out_specs=(PartitionSpec("layer", None, None), PartitionSpec("layer", "rep", None), PartitionSpec("rep")),
        check_vma=False,
    )
```

```python
import functools

import jax
import jax.numpy as jnp
from jax import lax
from jax.experimental import pallas as pl
from jax.experimental.pallas import tpu as pltpu
from jax.sharding import PartitionSpec

BAL = 32
BLOCK = 128
GROUP = 32
DAMPING = 0.05
F32 = jnp.float32
BF16 = jnp.bfloat16
VMEM = pl.BlockSpec(memory_space=pltpu.VMEM)


def split(x):
    hi = x.astype(BF16)
    lo = (x - hi.astype(F32)).astype(BF16)
    return hi, lo


def dot_t(a, b):
    return lax.dot_general(a, b, (((0,), (0,)), ((), ())), preferred_element_type=F32)


def dot(a, b):
    return lax.dot_general(a, b, (((1,), (0,)), ((), ())), preferred_element_type=F32)


def iota(shape, axis):
    return lax.broadcasted_iota(jnp.int32, shape, axis)


def onehot(mask, dtype=BF16):
    return jnp.where(mask, 1.0, 0.0).astype(dtype)

CHUNKS = (64, 128, 128, 128, 64)
AHEAD = 2


def project(block, proj):
    contract = (((1,), (1,)), ((), ()))
    return lax.dot_general(block, proj, contract, preferred_element_type=F32).astype(BF16)


def expand(x, pattern):
    return dot(x, pattern)


def front_kernel(
    acts_hbm, grads_hbm, in_hbm, out_hbm, segs_hbm, moves_hbm, arr_ref, aux_ref,
    acts, grads, in_proj, out_proj, segs, moves_in, sums, counts, moves_pad, sem, small_sem,
):
    replica = lax.axis_index("rep")
    kin, kout = in_proj.shape[0], out_proj.shape[0]
    slots, width = sums.shape
    doc_slots = moves_in.shape[1]
    small = [
        pltpu.make_async_copy(a, b, small_sem.at[i])
        for i, (a, b) in enumerate(
            ((in_hbm, in_proj), (out_hbm, out_proj), (segs_hbm, segs), (moves_hbm, moves_in))
        )
    ]
    large = []
    ends = [sum(CHUNKS[: c + 1]) for c in range(len(CHUNKS))]
    for c, size in enumerate(CHUNKS):
        rows = pl.ds(ends[c] - size, size)
        large.append(
            (
                pltpu.make_async_copy(acts_hbm.at[rows], acts.at[rows], sem.at[0, c]),
                pltpu.make_async_copy(grads_hbm.at[rows], grads.at[rows], sem.at[1, c]),
            )
        )
    small[0].start()
    small[1].start()
    for pair in large[:AHEAD]:
        pair[0].start()
        pair[1].start()
    small[2].start()
    small[3].start()
    lane, sub = iota((kin, width), 1), iota((kin, width), 0)
    spread = onehot(lane // kout == sub)
    lane, sub = iota((kout, width), 1), iota((kout, width), 0)
    repeat = onehot(lane % kout == sub)
    moves_pad[...] = jnp.full_like(moves_pad, -1)
    def gather_documents(c, left, right):
        hi, lo = split(expand(left, spread) * expand(right, repeat))
        size = CHUNKS[c]
        here = segs[:, ends[c] - size : ends[c]]
        slot = iota((slots, size), 0)
        slot = jnp.where(slot == doc_slots, -1, slot)
        member = onehot(slot == here, F32)
        member_low = member.astype(BF16)
        twice = jnp.concatenate([member_low, member_low], axis=1)
        part = dot(twice, jnp.concatenate([hi, lo], axis=0))
        number = jnp.broadcast_to(jnp.sum(member, axis=1, keepdims=True), counts.shape)
        if c == 0:
            sums[...] = part
            counts[...] = number
        else:
            sums[...] += part
            counts[...] += number

    held = None
    for copy in small:
        copy.wait()
    for c, size in enumerate(CHUNKS):
        rows = pl.ds(ends[c] - size, size)
        for copy in large[c]:
            copy.wait()
        if c + AHEAD < len(CHUNKS):
            for copy in large[c + AHEAD]:
                copy.start()
        left = project(acts[rows, :], in_proj[...])
        right = project(grads[rows, :], out_proj[...])
        if c > 0:
            gather_documents(c - 1, *held)
        held = left, right
    gather_documents(len(CHUNKS) - 1, *held)
    moves_pad[:, :doc_slots] = moves_in[...]
    total, count = sums[...], counts[...]
    moves = moves_pad[...]
    last = jnp.max(segs[...], axis=1, keepdims=True)
    lanes = moves.shape[1]
    scale = 1.0 / jnp.sqrt(jnp.maximum(count, 1.0))
    scale = jnp.concatenate([scale] * (width // scale.shape[1]), axis=1)
    local = (total * scale).astype(BF16)
    local = jnp.concatenate([local, jnp.zeros((lanes - slots, width), BF16)], axis=0)
    row, slot = iota((3 * BAL, lanes), 0), iota((3 * BAL, lanes), 1)
    offset = jnp.where(row < BAL, 0, jnp.where(row < 2 * BAL, -1, 1))
    target = (replica + offset) * BAL + row % BAL
    chosen = (moves == target) & (moves >= 0) & (slot != last)
    arr_ref[...] = dot(onehot(chosen), local).astype(BF16)
    is_last = iota((slots, width), 0) == last
    last_sum = jnp.sum(jnp.where(is_last, total, 0.0), axis=0, keepdims=True)
    is_last = iota(counts.shape, 0) == last
    last_count = jnp.sum(jnp.where(is_last, count, 0.0), axis=0, keepdims=True)
    goes_to = jnp.sum(jnp.where(iota(moves.shape, 1) == last, moves, 0), axis=1, keepdims=True)
    tail = iota((8, 128), 0)
    facts = jnp.where(tail == 0, last_count, jnp.where(tail == 1, count[doc_slots : doc_slots + 1], goes_to.astype(F32)))
    folded = [
        v[:, 128 * i : 128 * i + 128]
        for v in (last_sum, total[doc_slots : doc_slots + 1])
        for i in range(width // 128)
    ]
    aux_ref[...] = jnp.concatenate(folded + [facts], axis=0)


def gather_kernel(side, cores, *refs):
    held, all_ref, work, refs = refs[:6], refs[6], refs[7:18], refs[18:]
    arr_ref, aux_ref, from_right, from_left, aux_in, ex_send, ex_recv, send, recv = refs
    n_rep = side * side * cores
    width = all_ref.shape[1]
    me = lax.axis_index("rep")
    core = me % cores
    spot_z = (me // cores) % side
    spot_x = me // (cores * side)

    def rep_at(dx, dz, c):
        x, z = (spot_x + dx + side) % side, (spot_z + dz + side) % side
        return (x * side + z) * cores + c

    right, left, left2 = (me + 1) % n_rep, (me + n_rep - 1) % n_rep, (me + n_rep - 2) % n_rep
    right2 = (me + 2) % n_rep
    sibling = rep_at(0, 0, 1 - core)
    around = [rep_at(d, 0, core) for d in (1, -1, 2)] + [rep_at(0, d, core) for d in (1, -1, 2)]
    barrier = pltpu.get_barrier_semaphore()
    senders = [right, left, right2, sibling] + around
    for device in senders:
        pl.semaphore_signal(barrier, inc=1, device_id={"rep": device}, device_id_type=pl.DeviceIdType.MESH)
    front_kernel(*held, arr_ref, aux_ref, *work)
    pl.semaphore_wait(barrier, len(senders))

    def copy(src, dst, s, r, device):
        return pltpu.make_async_remote_copy(
            src_ref=src, dst_ref=dst, send_sem=s, recv_sem=r,
            device_id={"rep": device}, device_id_type=pl.DeviceIdType.MESH,
        )

    first = [
        copy(aux_ref, aux_in.at[0], ex_send.at[0], ex_recv.at[0], left),
        copy(aux_ref, aux_in.at[1], ex_send.at[1], ex_recv.at[1], right),
        copy(aux_ref, aux_in.at[2], ex_send.at[2], ex_recv.at[2], left2),
        copy(arr_ref.at[pl.ds(BAL, BAL)], from_right, ex_send.at[3], ex_recv.at[3], left),
        copy(arr_ref.at[pl.ds(2 * BAL, BAL)], from_left, ex_send.at[4], ex_recv.at[4], right),
    ]
    for c in first:
        c.start()
    for c in first:
        c.wait_recv()

    mine = arr_ref[pl.ds(0, BAL), :].astype(F32) + from_right[...].astype(F32) + from_left[...].astype(F32)
    own = aux_ref[...]
    after, before, after2 = aux_in[0], aux_in[1], aux_in[2]
    row = iota((BAL, width), 0).astype(F32)
    base = (me * BAL).astype(F32)
    folds = width // 128
    for a, b in ((before, own), (own, after), (after, after2)):
        facts_a, facts_b = a[2 * folds :], b[2 * folds :]
        length = jnp.maximum(facts_a[0:1] + facts_b[1:2], 1.0)
        feature = (a[:folds] + b[folds : 2 * folds]) * (1.0 / jnp.sqrt(length))
        feature = jnp.concatenate([feature[i : i + 1] for i in range(folds)], axis=1)
        mine = jnp.where(row == facts_a[2:3, :1] - base, feature, mine)
    all_ref[pl.ds(pl.multiple_of(me * BAL, BAL), BAL), :] = mine.astype(BF16)

    half = width // 2
    sent = []

    def piece(dx, dz, c, col, cols):
        start = pl.multiple_of(rep_at(dx, dz, c) * BAL, BAL)
        return all_ref.at[pl.ds(start, BAL), pl.ds(col, cols)]

    def start(index, dx, dz, col, cols, device):
        ref = piece(dx, dz, core, col, cols)
        c = copy(ref, ref, send.at[index], recv.at[index], device)
        c.start()
        sent.append(c)

    def arrived(index, dx, dz, c, col, cols):
        ref = piece(dx, dz, c, col, cols)
        copy(ref, ref, send.at[index], recv.at[index], sibling).wait_recv()

    def place(kind, du, dv):
        return (du, dv) if kind == 0 else (dv, du)

    def to(kind, du, dv):
        return rep_at(*place(kind, du, dv), core)

    order = (0, 1, -1, 2)
    per_kind = 3 + 12 + 16

    def along(kind):
        for i, d in enumerate(order[1:]):
            start(kind * per_kind + i, 0, 0, kind * half, half, to(kind, d, 0))

    def across(kind, du):
        at = place(kind, du, 0)
        for i, d in enumerate(order[1:]):
            n = kind * per_kind + 3 + 3 * order.index(du) + i
            start(n, *at, kind * half, half, to(kind, 0, d))

    def share(kind, du, dv):
        n = kind * per_kind + 15 + 4 * order.index(du) + order.index(dv)
        start(n, *place(kind, du, dv), kind * half, half, sibling)

    def back(d):
        return d if d == 2 else -d

    for kind in (0, 1):
        along(kind)
    for kind in (0, 1):
        across(kind, 0)
        share(kind, 0, 0)
    for i, d in enumerate(order[1:]):
        for kind in (0, 1):
            arrived(kind * per_kind + i, *place(kind, back(d), 0), core, kind * half, half)
            across(kind, back(d))
            share(kind, back(d), 0)
    for du in (0, -1, 1, 2):
        for i, d in enumerate(order[1:]):
            for kind in (0, 1):
                n = kind * per_kind + 3 + 3 * order.index(du) + i
                arrived(n, *place(kind, du, back(d)), core, kind * half, half)
                share(kind, du, back(d))
    for kind in (0, 1):
        for i, du in enumerate(order):
            for j, dv in enumerate(order):
                n = kind * per_kind + 15 + 4 * i + j
                arrived(n, *place(kind, du, dv), 1 - core, kind * half, half)
    for c in first + sent:
        c.wait_send()


def gather(acts, grads, in_proj, out_proj, segs, moves, n_rep):
    kin, kout = in_proj.shape[0], out_proj.shape[0]
    width = kin * kout
    slots = -(-(moves.shape[1] + 1) // 16) * 16
    cores = 2
    side = round((n_rep // cores) ** 0.5)
    held = [
        pltpu.with_memory_space_constraint(v, pltpu.HBM)
        for v in (acts, grads, in_proj, out_proj, segs, moves)
    ]
    return pl.pallas_call(
        functools.partial(gather_kernel, side, cores),
        out_shape=jax.ShapeDtypeStruct((BAL * n_rep, width), BF16),
        in_specs=[pl.BlockSpec(memory_space=pltpu.HBM)] * 6,
        out_specs=VMEM,
        scratch_shapes=[
            pltpu.VMEM(acts.shape, BF16),
            pltpu.VMEM(grads.shape, BF16),
            pltpu.VMEM(in_proj.shape, BF16),
            pltpu.VMEM(out_proj.shape, BF16),
            pltpu.VMEM(segs.shape, jnp.int32),
            pltpu.VMEM(moves.shape, jnp.int32),
            pltpu.VMEM((slots, width), F32),
            pltpu.VMEM((slots, 128), F32),
            pltpu.VMEM((1, 128), jnp.int32),
            pltpu.SemaphoreType.DMA((2, len(CHUNKS))),
            pltpu.SemaphoreType.DMA((4,)),
            pltpu.VMEM((3 * BAL, width), BF16),
            pltpu.VMEM((width // 64 + 8, 128), F32),
            pltpu.VMEM((BAL, width), BF16),
            pltpu.VMEM((BAL, width), BF16),
            pltpu.VMEM((3, width // 64 + 8, 128), F32),
            pltpu.SemaphoreType.DMA((5,)),
            pltpu.SemaphoreType.DMA((5,)),
            pltpu.SemaphoreType.DMA((62,)),
            pltpu.SemaphoreType.DMA((62,)),
        ],
        compiler_params=pltpu.CompilerParams(
            collective_id=0, has_side_effects=True, vmem_limit_bytes=40 * 2**20
        ),
    )(*held)

AHEAD_COLS = 6
SUB = 8

def pivot_rows(V, at):
    size, width = V.shape
    tiles, strips = size // 8, width // 128
    row = iota((8, 128), 0)
    rows = [[V[8 * i : 8 * i + 8, 128 * c : 128 * c + 128] for c in range(strips)] for i in range(tiles)]
    pivots = [jnp.ones((8, 128), F32) for _ in range(tiles)]
    cols = {}

    def element(column, j):
        return jnp.broadcast_to(column[j // 8][j % 8 : j % 8 + 1], (8, 128))

    def spread(first, stop):
        for k in range(first, stop):
            lanes = slice(at + k, at + k + 1)
            cols[k] = [
                jnp.broadcast_to(rows[i][0][:, lanes], (8, 128)) if i >= k // 8 else None for i in range(tiles)
            ]

    for j in range(0, size, 2):
        tile, sub = divmod(j, 8)
        end = j - j % SUB + SUB
        if j == 0:
            spread(0, SUB)
        if j == end - AHEAD_COLS and end < size:
            spread(end, end + SUB)
        one, two = cols[j], cols[j + 1]
        p, q, r = element(one, j), element(one, j + 1), element(two, j + 1)
        det = p * r - q * q
        inv_p = 1.0 / p
        inv_det = 1.0 / det
        ratio = q * inv_p
        second = p * inv_det
        pivots[tile] = jnp.where(row == sub, p, pivots[tile])
        pivots[tile] = jnp.where(row == sub + 1, det * inv_p, pivots[tile])
        left = [None] * tiles
        right = [None] * tiles
        rest = [None] * tiles
        for i in range(tile, tiles):
            rest[i] = two[i] - one[i] * ratio
            left[i] = one[i] * inv_p
            right[i] = rest[i] * second
        for j2 in [k for k in sorted(cols) if k > j + 1]:
            mul_one, mul_two = element(one, j2), element(rest, j2)
            for i in range(j2 // 8, tiles):
                cols[j2][i] = (cols[j2][i] - left[i] * mul_one) - right[i] * mul_two
        for c in range(strips):
            top = jnp.broadcast_to(rows[tile][c][sub : sub + 1], (8, 128))
            next_row = jnp.broadcast_to(rows[tile][c][sub + 1 : sub + 2], (8, 128)) - top * ratio
            for i in range(tile, tiles):
                if i == tile:
                    wl = jnp.where(row > sub, left[i], 0.0)
                    wr = jnp.where(row > sub + 1, right[i], 0.0)
                else:
                    wl, wr = left[i], right[i]
                rows[i][c] = (rows[i][c] - wl * top) - wr * next_row
    out = []
    for i in range(tiles):
        scale = lax.rsqrt(pivots[i])
        out.append(jnp.concatenate([rows[i][c] * scale for c in range(strips)], axis=1))
    return jnp.concatenate(out, axis=0)


def factor_block(A):
    same = iota((BLOCK, BLOCK), 0) == iota((BLOCK, BLOCK), 1)
    V = jnp.concatenate([A, onehot(same, F32)], axis=1)
    done = []
    for at in range(0, BLOCK, GROUP):
        rows = pivot_rows(V[:GROUP], at)
        done.append(rows)
        if at + GROUP < BLOCK:
            hi, lo = split(rows)
            here = jnp.concatenate([hi, hi, lo], axis=0)
            update = dot_t(here[:, :BLOCK], jnp.concatenate([hi, lo, hi], axis=0))
            V = V[GROUP:] - update[at + GROUP :]
    both = jnp.concatenate(done, axis=0)
    return both[:, :BLOCK], both[:, BLOCK:]


def product(lh, ll, gh, gl):
    left = jnp.concatenate([lh, lh, ll], axis=0)
    return dot_t(left, jnp.concatenate([gh, gl, gh], axis=0))


def solve(inverse, columns):
    th, tl = split(inverse)
    sh, sl = split(columns)
    return dot(jnp.concatenate([th, th, tl], axis=1), jnp.concatenate([sh, sl, sh], axis=0))


def factor_kernel(all_ref, fac_hbm, mine_hbm, quad_ref, fac_ref, high, low, sem):
    docs, n = all_ref.shape
    width = n + 128
    replica = lax.axis_index("rep")
    own = pl.ds(pl.multiple_of(replica * BAL, BAL), BAL)
    mine = all_ref[own, :]
    writes = [pltpu.make_async_copy(all_ref.at[own], mine_hbm, sem.at[n // BLOCK])]
    writes[0].start()
    ri, ci = iota((BLOCK, BLOCK), 0), iota((BLOCK, BLOCK), 1)
    quad = jnp.zeros((1, 128), F32)

    def open_panel(a):
        b, before = a + BLOCK, a - BLOCK
        left = all_ref[:, a:b]
        hessian = dot_t(left, left)
        if b < n:
            hessian = jnp.concatenate([hessian, dot_t(left, all_ref[:, b:n])], axis=1)
        hessian = hessian * (1.0 / docs)
        extra = mine[:, a:b].astype(F32).T
        extra = jnp.concatenate([extra, jnp.zeros((BLOCK, 128 - BAL), F32)], axis=1)
        panel = jnp.concatenate([hessian, extra], axis=1)
        if before > 0:
            lh, ll = high[:before, a:b], low[:before, a:b]
            gh, gl = high[:before, a:width], low[:before, a:width]
            panel = panel - (dot_t(lh, gh) + dot_t(lh, gl) + dot_t(ll, gh))
        return panel

    following = open_panel(0)
    for a in range(0, n, BLOCK):
        b = a + BLOCK
        diag, rest = following[:, :BLOCK], following[:, BLOCK:]
        if a > 0:
            lh, ll = hi[:, :BLOCK], lo[:, :BLOCK]
            diag = diag - product(lh, ll, lh, ll)
        if b < n:
            following = open_panel(b)
        upper, inverse = factor_block(diag + jnp.where(ri == ci, DAMPING, 0.0))
        if a > 0:
            rest = rest - product(lh, ll, hi[:, BLOCK:], lo[:, BLOCK:])
        fac_ref[a:b, a:b] = jnp.where(ci >= ri, upper, 0.0)
        parts = [solve(inverse, rest[:, :BLOCK])]
        if b < n:
            parts.append(solve(inverse, rest[:, BLOCK:]))
        solved = jnp.concatenate(parts, axis=1)
        if b < n:
            fac_ref[a:b, b:n] = solved[:, : n - b]
            hi, lo = split(solved)
            high[a:b, b:width] = hi
            low[a:b, b:width] = lo
        if a > 0:
            fac_ref[a:b, :a] = jnp.zeros((BLOCK, a), F32)
        done = pl.ds(a, BLOCK)
        writes.append(pltpu.make_async_copy(fac_ref.at[done], fac_hbm.at[done], sem.at[a // BLOCK]))
        writes[-1].start()
        tail = solved[:, n - b :]
        quad = quad + jnp.sum(tail * tail, axis=0, keepdims=True)
    quad_ref[...] = jnp.broadcast_to(quad * (1.0 / n), quad_ref.shape)
    for write in writes:
        write.wait()


def factor(everyone):
    docs, n = everyone.shape
    return pl.pallas_call(
        factor_kernel,
        out_shape=(
            jax.ShapeDtypeStruct((n, n), F32),
            jax.ShapeDtypeStruct((BAL, n), BF16),
            jax.ShapeDtypeStruct((8, 128), F32),
        ),
        in_specs=[VMEM],
        out_specs=(pl.BlockSpec(memory_space=pltpu.HBM), pl.BlockSpec(memory_space=pltpu.HBM), VMEM),
        scratch_shapes=[
            pltpu.VMEM((n, n), F32),
            pltpu.VMEM((n, n + 128), BF16),
            pltpu.VMEM((n, n + 128), BF16),
            pltpu.SemaphoreType.DMA((n // BLOCK + 1,)),
        ],
        compiler_params=pltpu.CompilerParams(vmem_limit_bytes=40 * 2**20),
    )(everyone)


def layer_sum_kernel(layers, quad_ref, out_ref, inbox, send, recv):
    me = lax.axis_index("layer")
    barrier = pltpu.get_barrier_semaphore()
    for step in range(1, layers):
        device = (me + step) % layers
        pl.semaphore_signal(barrier, inc=1, device_id={"layer": device}, device_id_type=pl.DeviceIdType.MESH)
    pl.semaphore_wait(barrier, layers - 1)
    copies = []
    for step in range(1, layers):
        copies.append(
            pltpu.make_async_remote_copy(
                src_ref=quad_ref, dst_ref=inbox.at[step - 1], send_sem=send.at[step - 1],
                recv_sem=recv.at[step - 1], device_id={"layer": (me + step) % layers},
                device_id_type=pl.DeviceIdType.MESH,
            )
        )
        copies[-1].start()
    total = quad_ref[...]
    for step, c in enumerate(copies):
        c.wait_recv()
        total = total + inbox[step]
    out_ref[...] = total[:1, :BAL]
    for c in copies:
        c.wait_send()


def layer_sum(quad, layers):
    return pl.pallas_call(
        functools.partial(layer_sum_kernel, layers),
        out_shape=jax.ShapeDtypeStruct((1, BAL), F32),
        in_specs=[VMEM],
        out_specs=VMEM,
        scratch_shapes=[
            pltpu.VMEM((layers - 1,) + quad.shape, F32),
            pltpu.SemaphoreType.DMA((layers - 1,)),
            pltpu.SemaphoreType.DMA((layers - 1,)),
        ],
        compiler_params=pltpu.CompilerParams(
            collective_id=1, has_side_effects=True, vmem_limit_bytes=2 * 2**20
        ),
    )(quad)


def on_device(n_rep, layers, activations, output_grads, in_projection, out_projection, segment_ids, move_list):
    everyone = gather(
        activations[0], output_grads[0], in_projection[0], out_projection[0],
        segment_ids[None], move_list[None], n_rep,
    )
    upper, mine, quad = factor(everyone)
    influence = layer_sum(quad, layers)
    return (upper[None], mine[None], influence[0])


def solution(mesh):
    placed = (
        PartitionSpec("layer", "rep", None),
        PartitionSpec("layer", "rep", None),
        PartitionSpec("layer", None, None),
        PartitionSpec("layer", None, None),
        PartitionSpec("rep"),
        PartitionSpec("rep"),
    )
    return jax.shard_map(
        functools.partial(on_device, mesh.shape["rep"], mesh.shape["layer"]),
        mesh=mesh,
        in_specs=placed,
        out_specs=(PartitionSpec("layer", None, None), PartitionSpec("layer", "rep", None), PartitionSpec("rep")),
        check_vma=False,
    )
```
